32 devices in a mesh: groups: 2 (over y), seq: 4 (over z), tp: 4 (over x, core).
Axes of the slice: x: 2, y: 2, z: 4, core: 2. Of those that a mesh axis runs over, the one named last changes fastest.
Arguments:
- query: bfloat16 [4096, 2048], P(('groups', 'seq'), 'tp'), parts along dimension 0, may hold values from -64 to 64
- key_head_rows: bfloat16 [4096, 512], P(('groups', 'seq'), 'tp'), parts along dimension 0, may hold values from -64 to 64
- value_head_rows: bfloat16 [4096, 512], P(('groups', 'seq'), 'tp'), parts along dimension 0, may hold values from -6 to 6
- output_gradient: bfloat16 [4096, 2048], P(('groups', 'seq'), 'tp'), parts along dimension 0, may hold values from -16 to 16
- doc_blocks: int32 [32, 8], P(('groups', 'seq')), parts along dimension 0, may hold values from 0 to 13, as said below
- w_query: bfloat16 [4096, 2048], P(None, 'tp'), may hold values from -0.5 to 0.5
- key_weight: bfloat16 [4096, 512], P(None, 'tp'), may hold values from -0.5 to 0.5
- value_weight: bfloat16 [4096, 512], P(None, 'tp'), may hold values from -0.5 to 0.5
Outputs:
- input_grad: bfloat16 [4096, 4096], P(('groups', 'seq'), 'tp'), parts along dimension 0
The draws below stay inside these ranges and needn't reach their ends.
There are 2 independent parts, one for each index of `groups`. The reference program is written for one: setup_inputs(seed, part) draws one part's arguments, and reference() takes and returns one part's arrays. A program takes and returns all parts, laid end to end along the dimension named above; an argument that names none is the same for every part. Nothing has to cross between parts.
Inputs may be any that keep to these rules, and one draw needn't show every extreme that they name: `doc_blocks`: row b holds max(b - o, 0) for 8 distinct offsets o of 2 to 12; every row b that starts a shard of 512 positions uses the offset 12, and the last row uses the offset 2.
All inputs are finite; a program needn't handle non-finite values.
Results may differ from the reference program's by a relative error of at most 0.014.
Values may be sent and summed in bfloat16 or wider, within the bound.
A program may use at most 128 MiB of HBM per device.

```python
import jax
import jax.numpy as jnp
from jax import lax

MODEL_WIDTH = 4096
QUERY_HEADS = 16
KEY_VALUE_HEADS = 4
HEAD_WIDTH = 128
BLOCK_POSITIONS = 128
LISTED_COUNT = 8
TOK_DEV = 512
TOKEN_COUNT = 2048
QUERY_BLOCK_COUNT = 16
SPAN_BLK = 12
N_TP = 4


def paired_rows(key):
    query_raw = jnp.clip(jax.random.normal(jax.random.fold_in(key, 11), (TOKEN_COUNT, QUERY_HEADS * HEAD_WIDTH), jnp.float32), -6.0, 6.0)
    key_unprojected = jnp.clip(jax.random.normal(jax.random.fold_in(key, 12), (TOKEN_COUNT, KEY_VALUE_HEADS * HEAD_WIDTH), jnp.float32), -6.0, 6.0)
    return (query_raw, key_unprojected)


def draw_query(key, part):
    return paired_rows(key)[0].astype(jnp.bfloat16)


def draw_key_head_rows(key, part):
    return paired_rows(key)[1].astype(jnp.bfloat16)


def draw_doc_blocks(key, part):
    option_count = SPAN_BLK - 1
    raw_scores = jax.random.randint(key, (QUERY_BLOCK_COUNT, option_count), 0, 1 << 20)
    sorted_scores = raw_scores * SPAN_BLK + jnp.arange(option_count)[None, :]
    row_index = jnp.arange(QUERY_BLOCK_COUNT)
    column_number = jnp.arange(option_count)[None, :]
    foremost_entries = row_index % (TOK_DEV // BLOCK_POSITIONS) == 0
    extra_score = jnp.where(foremost_entries[:, None] & (column_number == option_count - 1), 1 << 30, 0)
    closing_row = row_index == QUERY_BLOCK_COUNT - 1
    extra_score = extra_score + jnp.where(closing_row[:, None] & (column_number == 0), 1 << 30, 0)
    highest_values, selected_blocks = lax.top_k(sorted_scores + extra_score, LISTED_COUNT)
    block_ids = row_index[:, None] - (selected_blocks + 2)
    return jnp.maximum(block_ids, 0).astype(jnp.int32)


def level_of(key, extent, shards, smallest, largest):
    loudness = 1.0
    for dim, blocks in shards:
        steps = jax.random.uniform(jax.random.fold_in(jax.random.fold_in(key, 6), dim), (blocks,), jnp.float32, smallest / len(shards), largest / len(shards))
        loudness = loudness * jnp.repeat(jnp.exp(steps), extent[dim] // blocks).reshape((-1,) + (1,) * (len(extent) - 1 - dim))
    return loudness


def centred(own_key, shape, scale, limit, pieces=(), kind=jnp.bfloat16):
    level = level_of(own_key, shape, pieces, -0.22, 0.18) if pieces else 1.0
    result = jax.random.normal(own_key, shape, jnp.float32) * scale * level
    return jnp.minimum(jnp.maximum(result, -limit), limit).astype(kind)


def setup_inputs(seed: int = 0, part: int = 0) -> dict:
    splits = jax.random.split(jax.random.key(seed), 9)
    part_keys = jax.random.split(jax.random.fold_in(splits[8], part), 9)
    query = draw_query(jax.random.fold_in(jax.random.fold_in(splits[8], part), 71), part)
    key_head_rows = draw_key_head_rows(jax.random.fold_in(jax.random.fold_in(splits[8], part), 71), part)
    value_head_rows = centred(part_keys[2], (TOKEN_COUNT, KEY_VALUE_HEADS * HEAD_WIDTH), 1.0, 6.0, ((0, 4), (1, 4)))
    output_gradient = centred(part_keys[3], (TOKEN_COUNT, QUERY_HEADS * HEAD_WIDTH), 4.0, 16.0, ((0, 4), (1, 4)))
    doc_blocks = draw_doc_blocks(jax.random.fold_in(jax.random.fold_in(splits[8], part), 71), part)
    w_query = centred(splits[5], (MODEL_WIDTH, QUERY_HEADS * HEAD_WIDTH), HEAD_WIDTH ** -0.5, 0.5, ((1, 4),))
    key_weight = centred(splits[6], (MODEL_WIDTH, KEY_VALUE_HEADS * HEAD_WIDTH), HEAD_WIDTH ** -0.5, 0.5, ((1, 4),))
    value_weight = centred(splits[7], (MODEL_WIDTH, KEY_VALUE_HEADS * HEAD_WIDTH), HEAD_WIDTH ** -0.5, 0.5, ((1, 4),))
    return dict(query=query, key_head_rows=key_head_rows, value_head_rows=value_head_rows, output_gradient=output_gradient, doc_blocks=doc_blocks, w_query=w_query, key_weight=key_weight, value_weight=value_weight)


def block_grads(query_block, grad_block, key_block, value_block, allowed):
    score_scale = HEAD_WIDTH ** -0.5
    query_full = query_block.astype(jnp.float32)
    grad_full = grad_block.astype(jnp.float32)
    key_full = key_block.astype(jnp.float32)
    value_full = value_block.astype(jnp.float32)
    scores = jnp.einsum("qhgd,khd->hgqk", query_full, key_full) * score_scale
    scores = jnp.where(allowed, scores, -jnp.inf)
    row_max = jnp.max(scores, axis=-1, keepdims=True)
    weights = jnp.where(allowed, jnp.exp(scores - row_max), 0.0)
    probability = weights / jnp.sum(weights, axis=-1, keepdims=True)
    prob_half = lax.optimization_barrier(probability.astype(jnp.bfloat16)).astype(jnp.float32)
    attended = jnp.einsum("hgqk,khd->qhgd", prob_half, value_full)
    row_delta = jnp.sum(grad_full * attended, axis=-1)
    prob_grad = jnp.einsum("qhgd,khd->hgqk", grad_full, value_full)
    score_grad = probability * (prob_grad - jnp.transpose(row_delta, (1, 2, 0))[..., None])
    score_half = lax.optimization_barrier(score_grad.astype(jnp.bfloat16)).astype(jnp.float32)
    query_grad = jnp.einsum("hgqk,khd->qhgd", score_half, key_full) * score_scale
    key_gradient = jnp.einsum("hgqk,qhgd->khd", score_half, query_full) * score_scale
    value_gradient = jnp.einsum("hgqk,qhgd->khd", prob_half, grad_full)
    return query_grad, key_gradient, value_gradient


def reference(query, key_head_rows, value_head_rows, output_gradient, doc_blocks, w_query, key_weight, value_weight):
    group_width = QUERY_HEADS // KEY_VALUE_HEADS
    listed_slot_count = LISTED_COUNT + 2
    query_block_rows = query.reshape(QUERY_BLOCK_COUNT, BLOCK_POSITIONS, KEY_VALUE_HEADS, group_width, HEAD_WIDTH)
    gradient_blocks = output_gradient.reshape(QUERY_BLOCK_COUNT, BLOCK_POSITIONS, KEY_VALUE_HEADS, group_width, HEAD_WIDTH)
    key_block_rows = key_head_rows.reshape(QUERY_BLOCK_COUNT, BLOCK_POSITIONS, KEY_VALUE_HEADS, HEAD_WIDTH)
    value_block_rows = value_head_rows.reshape(QUERY_BLOCK_COUNT, BLOCK_POSITIONS, KEY_VALUE_HEADS, HEAD_WIDTH)
    offsets = jnp.arange(BLOCK_POSITIONS, dtype=jnp.int32)
    earlier = jnp.arange(LISTED_COUNT)[:, None] > jnp.arange(LISTED_COUNT)[None, :]
    far_slot = jnp.repeat(jnp.arange(listed_slot_count) >= 2, BLOCK_POSITIONS)

    def visit_block(sums_carry, block_id):
        key_gradient_sum, value_gradient_sum = sums_carry
        listed = doc_blocks[block_id].astype(jnp.int32)
        repeated = jnp.any((listed[:, None] == listed[None, :]) & earlier, axis=1)
        listed_ok = (listed <= block_id - 2) & jnp.logical_not(repeated)
        band_ids = jnp.stack([block_id - 1, block_id]).astype(jnp.int32)
        slot_ids = jnp.concatenate([band_ids, listed])
        slot_ok = jnp.concatenate([jnp.stack([block_id >= 1, block_id >= 0]), listed_ok])
        clamped_index = jnp.maximum(slot_ids, 0)
        query_pos = block_id * BLOCK_POSITIONS + offsets
        key_pos = (slot_ids[:, None] * BLOCK_POSITIONS + offsets[None, :]).reshape(-1)
        in_reach = (key_pos[None, :] <= query_pos[:, None]) & (query_pos[:, None] - key_pos[None, :] < BLOCK_POSITIONS)
        allowed = jnp.repeat(slot_ok, BLOCK_POSITIONS)[None, :] & (far_slot[None, :] | in_reach)
        present_keys = key_block_rows[clamped_index].reshape(listed_slot_count * BLOCK_POSITIONS, KEY_VALUE_HEADS, HEAD_WIDTH)
        present_values = value_block_rows[clamped_index].reshape(listed_slot_count * BLOCK_POSITIONS, KEY_VALUE_HEADS, HEAD_WIDTH)
        query_grad, key_gradient, value_gradient = block_grads(query_block_rows[block_id], gradient_blocks[block_id], present_keys, present_values, allowed)
        key_gradient_sum = key_gradient_sum.at[clamped_index].add(key_gradient.reshape(listed_slot_count, BLOCK_POSITIONS, KEY_VALUE_HEADS, HEAD_WIDTH))
        value_gradient_sum = value_gradient_sum.at[clamped_index].add(value_gradient.reshape(listed_slot_count, BLOCK_POSITIONS, KEY_VALUE_HEADS, HEAD_WIDTH))
        return (key_gradient_sum, value_gradient_sum), query_grad.astype(jnp.bfloat16)

    initial_zeros = jnp.zeros((QUERY_BLOCK_COUNT, BLOCK_POSITIONS, KEY_VALUE_HEADS, HEAD_WIDTH), jnp.float32)
    closing_sums, query_grads = lax.scan(visit_block, (initial_zeros, initial_zeros), jnp.arange(QUERY_BLOCK_COUNT, dtype=jnp.int32))
    query_grad_all = query_grads.reshape(TOKEN_COUNT, QUERY_HEADS * HEAD_WIDTH)
    key_gradient_total = closing_sums[0].reshape(TOKEN_COUNT, KEY_VALUE_HEADS * HEAD_WIDTH).astype(jnp.bfloat16)
    value_gradient_total = closing_sums[1].reshape(TOKEN_COUNT, KEY_VALUE_HEADS * HEAD_WIDTH).astype(jnp.bfloat16)
    query_cols = QUERY_HEADS * HEAD_WIDTH // N_TP
    key_value_columns = KEY_VALUE_HEADS * HEAD_WIDTH // N_TP
    summed = jnp.zeros((TOKEN_COUNT, MODEL_WIDTH), jnp.float32)
    for shard_index in range(N_TP):
        query_span = slice(shard_index * query_cols, (shard_index + 1) * query_cols)
        kv_span = slice(shard_index * key_value_columns, (shard_index + 1) * key_value_columns)
        grad_term = jnp.dot(query_grad_all[:, query_span], w_query[:, query_span].T, preferred_element_type=jnp.float32)
        grad_term = grad_term + jnp.dot(key_gradient_total[:, kv_span], key_weight[:, kv_span].T, preferred_element_type=jnp.float32)
        grad_term = grad_term + jnp.dot(value_gradient_total[:, kv_span], value_weight[:, kv_span].T, preferred_element_type=jnp.float32)
        summed = summed + lax.optimization_barrier(grad_term.astype(jnp.bfloat16)).astype(jnp.float32)
    return summed.astype(jnp.bfloat16)
```

```python
import functools
import math

import jax
import jax.numpy as jnp
from jax import lax
from jax.experimental import pallas as pl
from jax.experimental.pallas import tpu as pltpu
from jax.sharding import PartitionSpec as P

HEAD_WIDTH = 128
BLOCK_POSITIONS = 128
MESH_ID = pl.DeviceIdType.MESH
SPARE_MIB = 12


def dot_t(a, b):
    return lax.dot_general(a, b, (((1,), (1,)), ((), ())), preferred_element_type=jnp.float32)


def dot_n(a, b):
    return lax.dot_general(a, b, (((1,), (0,)), ((), ())), preferred_element_type=jnp.float32)


def dot_lt(a, b):
    return lax.dot_general(a, b, (((0,), (0,)), ((), ())), preferred_element_type=jnp.float32)


FLOOR = -1e9


def attention_kernel(
    shards,
    reach,
    places,
    groups,
    q_hbm,
    k_hbm,
    v_hbm,
    g_hbm,
    docs_ref,
    wq_hbm,
    wk_hbm,
    wv_hbm,
    out_ref,
    q_ref,
    k_ref,
    v_ref,
    g_ref,
    dq_ref,
    dkv_ref,
    dkv_now,
    dkv_all,
    wk_all,
    wv_all,
    wq_ref,
    wk_ref,
    wv_ref,
    near_sum,
    pair_out,
    pair_in,
    far_out,
    far_in,
    load_sem,
    weight_sem,
    pair_send,
    pair_recv,
    far_send,
    far_recv,
    fetch_send,
    fetch_recv,
    relay_send,
    relay_recv,
    gather_send,
    gather_recv,
    kv_win,
    q_heads,
    g_heads,
    stats,
    delta,
    dq_sum,
    probs,
    kv_sum,
    ret_out,
    ret_in,
    send_sem,
    recv_sem,
    ret_send,
    ret_recv,
):
    B = BLOCK_POSITIONS
    rows = k_ref.shape[0]
    nb = rows // B
    heads = q_ref.shape[1] // HEAD_WIDTH
    listed_count = docs_ref.shape[1]
    me = lax.axis_index("seq")
    scale = HEAD_WIDTH ** -0.5
    scale2 = scale * math.log2(math.e)
    has_next = me + 1 < shards
    has_prev = me >= 1

    pairs = places // 2
    place = lax.axis_index("tp")
    my_pair = place // 2
    parity = place % 2
    partner = my_pair * 2 + 1 - parity
    cols = out_ref.shape[1]
    relayed = groups == 2
    group = lax.axis_index("groups")

    def peer_of(k):
        return lax.rem(my_pair + k, pairs) * 2 + parity

    def owner_of(k, mine):
        return lax.rem(my_pair + k, pairs) * 2 + (parity if mine else 1 - parity)

    loads = [
        pltpu.make_async_copy(src, dst, load_sem.at[n])
        for n, (src, dst) in enumerate(((k_hbm, k_ref), (q_hbm, q_ref), (v_hbm, v_ref), (g_hbm, g_ref)))
    ]
    for copy in loads:
        copy.start()

    barrier = pltpu.get_barrier_semaphore()
    others = [(k, m) for k in range(pairs) for m in range(2) if (k, m) != (0, 0)]
    for k, m in others:
        pl.semaphore_signal(barrier, inc=1, device_id={"tp": owner_of(k, m == 0)}, device_id_type=MESH_ID)
    if relayed:
        pl.semaphore_signal(barrier, inc=1, device_id={"groups": 1 - group}, device_id_type=MESH_ID)

    @pl.when(has_next)
    def _():
        pl.semaphore_signal(barrier, inc=1, device_id={"seq": me + 1}, device_id_type=MESH_ID)

    @pl.when(has_prev)
    def _():
        pl.semaphore_signal(barrier, inc=1, device_id={"seq": me - 1}, device_id_type=MESH_ID)

    greeted = places - 1 + (1 if relayed else 0)
    pl.semaphore_wait(barrier, has_next.astype(jnp.int32) + has_prev.astype(jnp.int32) + greeted)

    def forward(d, c):
        src = (k_hbm, v_hbm)[c] if d == 0 else kv_win.at[d - 1, c]
        return pltpu.make_async_remote_copy(
            src_ref=src,
            dst_ref=kv_win.at[d, c],
            send_sem=send_sem.at[d, c],
            recv_sem=recv_sem.at[d, c],
            device_id={"seq": jnp.minimum(me + 1, shards - 1)},
            device_id_type=MESH_ID,
        )

    def backward(d, c):
        return pltpu.make_async_remote_copy(
            src_ref=ret_out.at[d - 1, c],
            dst_ref=ret_in.at[d - 1, c],
            send_sem=ret_send.at[d - 1, c],
            recv_sem=ret_recv.at[d - 1, c],
            device_id={"seq": jnp.maximum(me - 1, 0)},
            device_id_type=MESH_ID,
        )

    def span_of(owner):
        return pl.ds(pl.multiple_of(owner * cols, cols), cols)

    def fetch(k, m, c):
        if isinstance(m, int):
            owner = owner_of(k, m == 0)
        else:
            owner = lax.rem(my_pair + k, pairs) * 2 + lax.rem(parity + m, 2)
        return pltpu.make_async_remote_copy(
            src_ref=(wk_hbm, wv_hbm)[c].at[span_of(owner)],
            dst_ref=(wk_all, wv_all)[c].at[k, m],
            send_sem=fetch_send.at[k, m, c],
            recv_sem=fetch_recv.at[k, m, c],
            device_id={"tp": owner},
            device_id_type=MESH_ID,
        )

    def relay(k, c):
        return pltpu.make_async_remote_copy(
            src_ref=(wk_all, wv_all)[c].at[k, group],
            dst_ref=(wk_all, wv_all)[c].at[k, group],
            send_sem=relay_send.at[k, c],
            recv_sem=relay_recv.at[k, c],
            device_id={"groups": 1 - group},
            device_id_type=MESH_ID,
        )

    def relay_in(k, c):
        return pltpu.make_async_remote_copy(
            src_ref=(wk_all, wv_all)[c].at[k, 1 - group],
            dst_ref=(wk_all, wv_all)[c].at[k, 1 - group],
            send_sem=relay_send.at[k, c],
            recv_sem=relay_recv.at[k, c],
            device_id={"groups": 1 - group},
            device_id_type=MESH_ID,
        )

    if relayed:
        fetches = [(0, 1, c) for c in range(2)] + [(k, group, c) for c in (1, 0) for k in range(1, pairs)]
    else:
        fetches = [(k, m, c) for k, m in others for c in range(2)]

    @pl.when(has_next)
    def _():
        forward(0, 0).start()
        forward(0, 1).start()
        for item in fetches:
            fetch(*item).start()

    whole = [
        pltpu.make_async_copy(wq_hbm, wq_ref, weight_sem.at[0]),
        pltpu.make_async_copy(wk_hbm, wk_ref, weight_sem.at[1]),
        pltpu.make_async_copy(wv_hbm, wv_ref, weight_sem.at[2]),
    ]
    for copy in whole:
        copy.start()

    width = heads * B
    for d in range(1, reach + 1):
        for i in range(nb):
            stats[d, i, 0:1, :] = jnp.full((1, width), FLOOR, jnp.float32)
            stats[d, i, 1:3, :] = jnp.zeros((2, width), jnp.float32)

    for copy in loads:
        copy.wait()
    for i in range(nb):
        for h in range(heads):
            q_heads[i, h * B : (h + 1) * B, :] = q_ref[i * B : (i + 1) * B, h * HEAD_WIDTH : (h + 1) * HEAD_WIDTH]
            g_heads[i, h * B : (h + 1) * B, :] = g_ref[i * B : (i + 1) * B, h * HEAD_WIDTH : (h + 1) * HEAD_WIDTH]
    key_row = lax.broadcasted_iota(jnp.int32, (B, width), 0)
    query_row = lax.broadcasted_iota(jnp.int32, (B, width), 1) & (B - 1)
    own_mask = key_row <= query_row

    def keys_of(d):
        if isinstance(d, int) and d == 0:
            return k_ref, v_ref
        return kv_win.at[d - 1, 0], kv_win.at[d - 1, 1]

    def key_span(d, i):
        if isinstance(i, int) and isinstance(d, int) and d == 0:
            return 0, i + 1
        if isinstance(i, int) and isinstance(d, int) and d == reach:
            return i, nb
        return 0, nb

    def biased(d, i, j, raw):
        offset = d * nb + i - j
        if isinstance(i, int) and offset == 0:
            return jnp.where(own_mask, raw, -jnp.inf), jnp.float32(0.0)
        if isinstance(i, int) and offset == 1:
            return jnp.where(own_mask, -jnp.inf, raw), jnp.float32(0.0)
        key_block = (me - d) * nb + j
        hits = jnp.int32(0)
        for n in range(listed_count):
            hits = hits | (docs_ref[i, n] == key_block).astype(jnp.int32)
        ok = (hits > 0) & (offset >= 2)
        return raw, jnp.where(ok, jnp.float32(0.0), jnp.float32(-jnp.inf))

    def raw_blocks(d, i):
        low, high = key_span(d, i)
        raw = dot_t(keys_of(d)[0][low * B : high * B, :], q_heads[i])
        return [
            biased(d, i, j, raw[(j - low) * B : (j - low + 1) * B]) for j in range(low, high)
        ]

    def score_step(d, i, fresh):
        low, high = key_span(d, i)
        blocks = raw_blocks(d, i)
        tops = [jnp.max(raw, axis=0, keepdims=True) * scale2 + bias for raw, bias in blocks]
        top = jnp.maximum(functools.reduce(jnp.maximum, tops), FLOOR)
        total = 0.0
        for j, (raw, bias) in enumerate(blocks):
            weight = jnp.exp2(raw * scale2 + (bias - top))
            total = total + jnp.sum(weight, axis=0, keepdims=True)
            probs[d, i, (low + j) * B : (low + j + 1) * B, :] = weight.astype(jnp.bfloat16)
        stats[d, i, 0:1, :] = top
        stats[d, i, 1:2, :] = total

    def delta_step(d, i, fresh):
        low, high = key_span(d, i)
        prob_grad = dot_t(keys_of(d)[1][low * B : high * B, :], g_heads[i])
        weight = probs[d, i, low * B : high * B, :].astype(jnp.float32)
        stats[d, i, 2:3, :] = jnp.sum(weight * prob_grad, axis=0, keepdims=True)

    def late_delta_step(d, i, fresh):
        delta_step(d, i, fresh)
        stats[d, i, 1:2, :] = jnp.ones((1, width), jnp.float32)

    def value_step(d, i, fresh):
        low, high = key_span(d, i)
        weight = probs[d, i, low * B : high * B, :].astype(jnp.float32)
        prob_half = (weight * stats[d, i, 1:2, :]).astype(jnp.bfloat16)
        probs[d, i, low * B : high * B, :] = prob_half
        term = dot_n(prob_half, g_heads[i])
        if fresh:
            kv_sum[d, 1, low * B : high * B, :] = term
        else:
            kv_sum[d, 1, low * B : high * B, :] += term

    def grad_step(d, i, fresh):
        low, high = key_span(d, i)
        keys = keys_of(d)[0][low * B : high * B, :]
        prob_grad = dot_t(keys_of(d)[1][low * B : high * B, :], g_heads[i])
        prob = probs[d, i, low * B : high * B, :].astype(jnp.float32)
        score_half = (prob * (prob_grad - delta[i, 0:1, :])).astype(jnp.bfloat16)
        term = dot_n(score_half, q_heads[i])
        if fresh:
            kv_sum[d, 0, low * B : high * B, :] = term
        else:
            kv_sum[d, 0, low * B : high * B, :] += term
        turned = dot_lt(keys, score_half)
        if isinstance(d, int) and d == 0:
            dq_sum[i] = turned
        else:
            dq_sum[i] += turned

    def over_blocks(d, step):
        if d == 0:
            for i in range(nb - 1, -1, -1):
                step(d, i, i == nb - 1)
            return
        step(d, 0, True)
        if d == reach:
            for i in range(1, nb):
                step(d, i, False)
            return

        def one(i, carry):
            step(d, i, False)
            return carry

        lax.fori_loop(1, nb, one, 0)

    def present(d, step, extra=None):
        @pl.when(me >= d if extra is None else (me >= d) & extra)
        def _():
            over_blocks(d, step)

    def arrive(d, c):
        @pl.when(me >= d)
        def _():
            forward(d - 1, c).wait_recv()

        if d < reach:

            @pl.when((me >= d) & has_next)
            def _():
                forward(d, c).start()

    def scaled(d, c):
        return kv_sum[d, c] * scale if c == 0 else kv_sum[d, c]

    def send_first(d, c):
        first = me >= d if d == reach else (me >= d) & jnp.logical_not(has_next)

        @pl.when(first)
        def _():
            ret_out[d - 1, c] = scaled(d, c).astype(jnp.bfloat16)
            backward(d, c).start()

    def send_on(d, c):
        @pl.when((me >= d) & has_next)
        def _():
            backward(d + 1, c).wait_recv()
            ret_out[d - 1, c] = (scaled(d, c) + ret_in[d, c].astype(jnp.float32)).astype(jnp.bfloat16)
            backward(d, c).start()

    present(0, score_step)
    present(0, delta_step)
    for d in range(1, reach + 1):
        arrive(d, 0)
        present(d, score_step)
        if d < reach:

            @pl.when(me > d)
            def _():
                forward(d - 1, 1).wait_recv()

                @pl.when(has_next)
                def _():
                    forward(d, 1).start()

                over_blocks(d, delta_step)

    for i in range(nb):
        tops = [stats[d, i, 0:1, :] for d in range(reach + 1)]
        top = functools.reduce(jnp.maximum, tops)
        parts = [jnp.exp2(t - top) for t in tops]
        total = functools.reduce(jnp.add, [parts[d] * stats[d, i, 1:2, :] for d in range(reach + 1)])
        inverse = 1.0 / total
        for d in range(reach + 1):
            stats[d, i, 1:2, :] = parts[d] * inverse

    for d in range(reach, -1, -1):
        present(d, value_step)
        if d > 0:
            send_first(d, 1)

    for d in range(1, reach + 1):

        @pl.when(me >= reach if d == reach else me == d)
        def _():
            forward(d - 1, 1).wait_recv()
            if d < reach:

                @pl.when(has_next)
                def _():
                    forward(d, 1).start()

            over_blocks(d, late_delta_step)

    for i in range(nb):
        delta[i, 0:1, :] = functools.reduce(
            jnp.add, [stats[d, i, 1:2, :] * stats[d, i, 2:3, :] for d in range(reach + 1)]
        )

    @pl.when(me >= reach)
    def _():
        kv_sum[reach, 0] = jnp.zeros((rows, HEAD_WIDTH), jnp.float32)

    def grads_of(i):
        grad_step(0, i, i == nb - 1)

        def one(d, carry):
            grad_step(d, i, i == nb - 1)
            return carry

        if reach > 1:
            lax.fori_loop(1, jnp.minimum(me, reach - 1) + 1, one, 0)

        @pl.when(me >= reach)
        def _():
            grad_step(reach, i, False)

        part = slice(i * B, (i + 1) * B)
        turned = (dq_sum[i] * scale).T.astype(jnp.bfloat16)
        for h in range(heads):
            dq_ref[part, h * HEAD_WIDTH : (h + 1) * HEAD_WIDTH] = turned[h * B : (h + 1) * B]
        for c in range(2):
            own = kv_sum[0, c, part, :] * scale if c == 0 else kv_sum[0, c, part, :]
            dkv_now[part, c * HEAD_WIDTH : (c + 1) * HEAD_WIDTH] = jnp.where(
                has_next, jnp.float32(0.0), own
            ).astype(jnp.bfloat16)

    chunks = nb
    step_rows = rows // chunks

    def term(owner, c):
        span = pl.ds(pl.multiple_of(owner * cols, cols), cols)
        part = slice(c * step_rows, (c + 1) * step_rows)
        value = dot_t(dq_ref[part, :], wq_ref[span, :])
        value = value + dot_t(dkv_now[part, :HEAD_WIDTH], wk_ref[span, :])
        return value + dot_t(dkv_now[part, HEAD_WIDTH:], wv_ref[span, :])

    def to_pair(k, c):
        return pltpu.make_async_remote_copy(
            src_ref=pair_out.at[k, c],
            dst_ref=pair_in.at[k, c],
            send_sem=pair_send.at[k, c],
            recv_sem=pair_recv.at[k, c],
            device_id={"tp": partner},
            device_id_type=MESH_ID,
        )

    def to_far(k, c):
        return pltpu.make_async_remote_copy(
            src_ref=far_out.at[k - 1, c],
            dst_ref=far_in.at[k - 1, c],
            send_sem=far_send.at[k - 1, c],
            recv_sem=far_recv.at[k - 1, c],
            device_id={"tp": peer_of(k)},
            device_id_type=MESH_ID,
        )

    def give(k, c):
        pair_out[k, c] = term(owner_of(k, False), c).astype(jnp.bfloat16)
        to_pair(k, c).start()

    def take(k, c):
        value = term(owner_of(k, True), c)
        to_pair(k, c).wait_recv()
        value = value + pair_in[k, c].astype(jnp.float32)
        if k == 0:
            near_sum[c] = value
        else:
            far_out[k - 1, c] = value.astype(jnp.bfloat16)
            to_far(k, c).start()

    def far_terms(c):
        for k in range(1, pairs):
            give(k, c)
        for k in range(1, pairs):
            take(k, c)

    grads_of(nb - 1)
    for copy in whole:
        copy.wait()
    far_terms(nb - 1)

    if relayed:

        @pl.when(has_next)
        def _():
            for c in (1, 0):
                for k in range(1, pairs):
                    fetch(k, group, c).wait_recv()
                    relay(k, c).start()

    for i in range(nb - 2, -1, -1):
        grads_of(i)
    for d in range(reach, 0, -1):
        send_first(d, 0)
    for i in range(nb - 2, -1, -1):
        far_terms(i)
    for d in range(reach - 1, 0, -1):
        send_on(d, 1)
    near = list(range(nb - 1, -1, -1))
    give(0, near[0])
    for n, c in enumerate(near):
        if n + 1 < len(near):
            give(0, near[n + 1])
        take(0, c)

    def gather(k, m, c):
        return pltpu.make_async_remote_copy(
            src_ref=dkv_all.at[k, 0, c] if m == 1 and k > 0 else dkv_ref.at[c],
            dst_ref=dkv_all.at[k, m, c],
            send_sem=gather_send.at[k, m, c],
            recv_sem=gather_recv.at[k, m, c],
            device_id={"tp": partner if m == 1 else peer_of(k)},
            device_id_type=MESH_ID,
        )

    def settle(c):
        @pl.when(has_next)
        def _():
            backward(1, c).wait_recv()
            dkv_ref[c] = (scaled(0, c) + ret_in[0, c].astype(jnp.float32)).astype(jnp.bfloat16)
            for k in range(1, pairs):
                gather(k, 0, c).start()
            gather(0, 1, c).start()

    def add_terms(pairs_of):
        for c in range(chunks):
            part = slice(c * step_rows, (c + 1) * step_rows)
            value = near_sum[c]
            for grads, w in pairs_of:
                value = value + dot_t(grads[part, :], w[...])
            near_sum[c] = value

    def near_adds(c):
        own = span_of(place)
        gather(0, 1, c).wait_recv()
        add_terms(
            [
                (dkv_ref.at[c], (wk_ref, wv_ref)[c].at[own]),
                (dkv_all.at[0, 1, c], (wk_all, wv_all)[c].at[0, 1]),
            ]
        )

    def far_adds(c):
        for k in range(1, pairs):
            gather(k, 0, c).wait_recv()
            gather(k, 1, c).start()
        for k in range(1, pairs):
            gather(k, 1, c).wait_recv()
            add_terms([(dkv_all.at[k, m, c], (wk_all, wv_all)[c].at[k, m]) for m in range(2)])

    settle(1)

    @pl.when(has_next)
    def _():
        for c in range(2):
            fetch(0, 1, c).wait_recv()
        near_adds(1)

    for d in range(reach - 1, 0, -1):
        send_on(d, 0)

    @pl.when(has_next)
    def _():
        for k in range(1, pairs):
            for c in range(2):
                if relayed:
                    relay_in(k, c).wait_recv()
                else:
                    for m in range(2):
                        fetch(k, m, c).wait_recv()
        far_adds(1)

    settle(0)

    @pl.when(has_next)
    def _():
        near_adds(0)
        far_adds(0)

    for c in near:
        value = near_sum[c]
        for k in range(1, pairs):
            to_far(k, c).wait_recv()
            value = value + far_in[k - 1, c].astype(jnp.float32)
        out_ref[c * step_rows : (c + 1) * step_rows, :] = value.astype(jnp.bfloat16)

    @pl.when(has_next)
    def _():
        for k, m in others:
            for c in range(2):
                gather(k, m, c).wait_send()
        for item in fetches:
            fetch(*item).wait_send()
        if relayed:
            for k in range(1, pairs):
                for c in range(2):
                    relay(k, c).wait_send()

    for c in near:
        for k in range(pairs):
            to_pair(k, c).wait_send()
            if k > 0:
                to_far(k, c).wait_send()

    for d in range(reach):

        @pl.when((me >= d) & has_next)
        def _():
            for c in range(2):
                forward(d, c).wait_send()

        @pl.when(me >= d + 1)
        def _():
            for c in range(2):
                backward(d + 1, c).wait_send()


def body(
    query,
    key_head_rows,
    value_head_rows,
    output_gradient,
    doc_blocks,
    w_query,
    key_weight,
    value_weight,
):
    shards = lax.axis_size("seq")
    places = lax.axis_size("tp")
    groups = lax.axis_size("groups")
    pairs = places // 2
    reach = min(8, shards - 1)
    rows, q_width = query.shape
    nb = rows // BLOCK_POSITIONS
    cols = w_query.shape[0] // places
    width = (q_width // HEAD_WIDTH) * BLOCK_POSITIONS
    half, full = jnp.bfloat16, jnp.float32
    vmem = pl.BlockSpec(memory_space=pltpu.VMEM)
    hbm = pl.BlockSpec(memory_space=pltpu.HBM)
    dma = pltpu.SemaphoreType.DMA
    buffers = [
        ((rows, q_width), half),
        ((rows, HEAD_WIDTH), half),
        ((rows, HEAD_WIDTH), half),
        ((rows, q_width), half),
        ((rows, q_width), half),
        ((2, rows, HEAD_WIDTH), half),
        ((rows, 2 * HEAD_WIDTH), half),
        ((pairs, 2, 2, rows, HEAD_WIDTH), half),
        ((pairs, 2, cols, HEAD_WIDTH), half),
        ((pairs, 2, cols, HEAD_WIDTH), half),
        (w_query.shape, half),
        (key_weight.shape, half),
        (value_weight.shape, half),
        ((nb, rows // nb, cols), full),
        ((pairs, nb, rows // nb, cols), half),
        ((pairs, nb, rows // nb, cols), half),
        ((pairs - 1, nb, rows // nb, cols), half),
        ((pairs - 1, nb, rows // nb, cols), half),
    ]
    later = [
        ((reach, 2, rows, HEAD_WIDTH), half),
        ((nb, width, HEAD_WIDTH), half),
        ((nb, width, HEAD_WIDTH), half),
        ((reach + 1, nb, 8, width), full),
        ((nb, 8, width), full),
        ((nb, HEAD_WIDTH, width), full),
        ((reach + 1, nb, rows, width), half),
        ((reach + 1, 2, rows, HEAD_WIDTH), full),
        ((reach, 2, rows, HEAD_WIDTH), half),
        ((reach, 2, rows, HEAD_WIDTH), half),
    ]
    used = sum(math.prod(shape) * jnp.dtype(kind).itemsize for shape, kind in buffers + later)
    limit = min(used + SPARE_MIB * 1024 * 1024, 60 * 1024 * 1024)
    return pl.pallas_call(
        functools.partial(attention_kernel, shards, reach, places, groups),
        out_shape=jax.ShapeDtypeStruct((rows, cols), half),
        in_specs=[hbm] * 4 + [pl.BlockSpec(memory_space=pltpu.SMEM)] + [hbm] * 3,
        out_specs=vmem,
        scratch_shapes=[pltpu.VMEM(*item) for item in buffers]
        + [
            dma((4,)),
            dma((3,)),
            dma((pairs, nb)),
            dma((pairs, nb)),
            dma((pairs - 1, nb)),
            dma((pairs - 1, nb)),
            dma((pairs, 2, 2)),
            dma((pairs, 2, 2)),
            dma((pairs, 2)),
            dma((pairs, 2)),
            dma((pairs, 2, 2)),
            dma((pairs, 2, 2)),
        ]
        + [pltpu.VMEM(*item) for item in later]
        + [
            dma((reach, 2)),
            dma((reach, 2)),
            dma((reach, 2)),
            dma((reach, 2)),
        ],
        compiler_params=pltpu.CompilerParams(
            collective_id=0, has_side_effects=True, vmem_limit_bytes=limit
        ),
        name="attention",
    )(
        pltpu.with_memory_space_constraint(query, pltpu.HBM),
        pltpu.with_memory_space_constraint(key_head_rows, pltpu.HBM),
        pltpu.with_memory_space_constraint(value_head_rows, pltpu.HBM),
        pltpu.with_memory_space_constraint(output_gradient, pltpu.HBM),
        doc_blocks,
        pltpu.with_memory_space_constraint(w_query, pltpu.HBM),
        pltpu.with_memory_space_constraint(key_weight, pltpu.HBM),
        pltpu.with_memory_space_constraint(value_weight, pltpu.HBM),
    )


def solution(mesh):
    in_specs = (
        P(("groups", "seq"), "tp"),
        P(("groups", "seq"), "tp"),
        P(("groups", "seq"), "tp"),
        P(("groups", "seq"), "tp"),
        P(("groups", "seq"), None),
        P(None, "tp"),
        P(None, "tp"),
        P(None, "tp"),
    )
    out_specs = P(("groups", "seq"), "tp")
    return jax.shard_map(body, mesh=mesh, in_specs=in_specs, out_specs=out_specs, check_vma=False)
```

```python
import functools
import math

import jax
import jax.numpy as jnp
from jax import lax
from jax.experimental import pallas as pl
from jax.experimental.pallas import tpu as pltpu
from jax.sharding import PartitionSpec as P

HEAD_WIDTH = 128
BLOCK_POSITIONS = 128
MESH_ID = pl.DeviceIdType.MESH
SPARE_MIB = 12


def dot_t(a, b):
    return lax.dot_general(a, b, (((1,), (1,)), ((), ())), preferred_element_type=jnp.float32)


def dot_n(a, b):
    return lax.dot_general(a, b, (((1,), (0,)), ((), ())), preferred_element_type=jnp.float32)


def dot_lt(a, b):
    return lax.dot_general(a, b, (((0,), (0,)), ((), ())), preferred_element_type=jnp.float32)


FLOOR = -1e9


def attention_kernel(
    shards,
    reach,
    places,
    groups,
    q_hbm,
    k_hbm,
    v_hbm,
    g_hbm,
    docs_hbm,
    wq_hbm,
    wk_hbm,
    wv_hbm,
    out_ref,
    docs_ref,
    q_ref,
    k_ref,
    v_ref,
    g_ref,
    dq_ref,
    dkv_now,
    dkv_all,
    kw_all,
    wq_ref,
    wk_ref,
    wv_ref,
    near_sum,
    pair_out,
    pair_in,
    far_out,
    far_in,
    load_sem,
    weight_sem,
    pair_send,
    pair_recv,
    far_send,
    far_recv,
    fetch_send,
    fetch_recv,
    relay_send,
    relay_recv,
    gather_send,
    gather_recv,
    kv_win,
    q_heads,
    g_heads,
    stats,
    delta,
    dq_sum,
    probs,
    kv_sum,
    ret_out,
    ret_in,
    send_sem,
    recv_sem,
    ret_send,
    ret_recv,
):
    B = BLOCK_POSITIONS
    rows = k_ref.shape[0]
    nb = rows // B
    heads = q_ref.shape[1] // HEAD_WIDTH
    listed_count = docs_ref.shape[1]
    me = lax.axis_index("seq")
    scale = HEAD_WIDTH ** -0.5
    scale2 = scale * math.log2(math.e)
    has_next = me + 1 < shards
    has_prev = me >= 1

    pairs = places // 2
    place = lax.axis_index("tp")
    my_pair = place // 2
    parity = place % 2
    partner = my_pair * 2 + 1 - parity
    cols = out_ref.shape[1]
    relayed = groups == 2
    group = lax.axis_index("groups")

    def peer_of(k):
        return lax.rem(my_pair + k, pairs) * 2 + parity

    def owner_of(k, mine):
        return lax.rem(my_pair + k, pairs) * 2 + (parity if mine else 1 - parity)

    loads = [
        pltpu.make_async_copy(src, dst, load_sem.at[n])
        for n, (src, dst) in enumerate(((k_hbm, k_ref), (q_hbm, q_ref), (v_hbm, v_ref), (g_hbm, g_ref), (docs_hbm, docs_ref)))
    ]
    for copy in loads:
        copy.start()

    barrier = pltpu.get_barrier_semaphore()
    others = [(k, m) for k in range(pairs) for m in range(2) if (k, m) != (0, 0)]
    for k, m in others:
        pl.semaphore_signal(barrier, inc=1, device_id={"tp": owner_of(k, m == 0)}, device_id_type=MESH_ID)
    if relayed:
        pl.semaphore_signal(barrier, inc=1, device_id={"groups": 1 - group}, device_id_type=MESH_ID)

    @pl.when(has_next)
    def _():
        pl.semaphore_signal(barrier, inc=1, device_id={"seq": me + 1}, device_id_type=MESH_ID)

    @pl.when(has_prev)
    def _():
        pl.semaphore_signal(barrier, inc=1, device_id={"seq": me - 1}, device_id_type=MESH_ID)

    greeted = places - 1 + (1 if relayed else 0)
    pl.semaphore_wait(barrier, has_next.astype(jnp.int32) + has_prev.astype(jnp.int32) + greeted)

    def forward(d, c):
        src = (k_hbm, v_hbm)[c] if d == 0 else kv_win.at[d - 1, c]
        return pltpu.make_async_remote_copy(
            src_ref=src,
            dst_ref=kv_win.at[d, c],
            send_sem=send_sem.at[d, c],
            recv_sem=recv_sem.at[d, c],
            device_id={"seq": jnp.minimum(me + 1, shards - 1)},
            device_id_type=MESH_ID,
        )

    def backward(d, c):
        return pltpu.make_async_remote_copy(
            src_ref=ret_out.at[d - 1, c],
            dst_ref=ret_in.at[d - 1, c],
            send_sem=ret_send.at[d - 1, c],
            recv_sem=ret_recv.at[d - 1, c],
            device_id={"seq": jnp.maximum(me - 1, 0)},
            device_id_type=MESH_ID,
        )

    def span_of(owner):
        return pl.ds(pl.multiple_of(owner * cols, cols), cols)

    def slot(k, m):
        lane = (2 * k + m) * HEAD_WIDTH
        return pl.ds(lane if isinstance(m, int) else pl.multiple_of(lane, HEAD_WIDTH), HEAD_WIDTH)

    def fetch(k, m, c):
        if isinstance(m, int):
            owner = owner_of(k, m == 0)
        else:
            owner = lax.rem(my_pair + k, pairs) * 2 + lax.rem(parity + m, 2)
        return pltpu.make_async_remote_copy(
            src_ref=(wk_hbm, wv_hbm)[c].at[span_of(owner)],
            dst_ref=kw_all.at[c, :, slot(k, m)],
            send_sem=fetch_send.at[k, m, c],
            recv_sem=fetch_recv.at[k, m, c],
            device_id={"tp": owner},
            device_id_type=MESH_ID,
        )

    def own_weights(c):
        return pltpu.make_async_copy(
            (wk_hbm, wv_hbm)[c].at[span_of(place)], kw_all.at[c, :, slot(0, 0)], fetch_recv.at[0, 0, c]
        )

    def relay(k, c, arriving=False):
        which = 1 - group if arriving else group
        return pltpu.make_async_remote_copy(
            src_ref=kw_all.at[c, :, slot(k, which)],
            dst_ref=kw_all.at[c, :, slot(k, which)],
            send_sem=relay_send.at[k, c],
            recv_sem=relay_recv.at[k, c],
            device_id={"groups": 1 - group},
            device_id_type=MESH_ID,
        )

    if relayed:
        fetches = [(0, 1, c) for c in range(2)] + [(k, group, c) for c in (1, 0) for k in range(1, pairs)]
    else:
        fetches = [(k, m, c) for k, m in others for c in range(2)]

    @pl.when(has_next)
    def _():
        forward(0, 0).start()
        forward(0, 1).start()
        for item in fetches:
            fetch(*item).start()
        for c in range(2):
            own_weights(c).start()

    whole = [
        pltpu.make_async_copy(wq_hbm, wq_ref, weight_sem.at[0]),
        pltpu.make_async_copy(wk_hbm, wk_ref, weight_sem.at[1]),
        pltpu.make_async_copy(wv_hbm, wv_ref, weight_sem.at[2]),
    ]
    for copy in whole:
        copy.start()

    width = heads * B
    for d in range(1, reach + 1):
        for i in range(nb):
            stats[d, i, 0:1, :] = jnp.full((1, width), FLOOR, jnp.float32)
            stats[d, i, 1:3, :] = jnp.zeros((2, width), jnp.float32)

    for i in range(nb):
        dq_sum[i] = jnp.zeros((HEAD_WIDTH, width), jnp.float32)

    @pl.when(me >= reach)
    def _():
        kv_sum[reach, 0] = jnp.zeros((rows, HEAD_WIDTH), jnp.float32)

    for copy in loads:
        copy.wait()
    for i in range(nb):
        for h in range(heads):
            q_heads[i, h * B : (h + 1) * B, :] = q_ref[i * B : (i + 1) * B, h * HEAD_WIDTH : (h + 1) * HEAD_WIDTH]
            g_heads[i, h * B : (h + 1) * B, :] = g_ref[i * B : (i + 1) * B, h * HEAD_WIDTH : (h + 1) * HEAD_WIDTH]
    key_row = lax.broadcasted_iota(jnp.int32, (B, width), 0)
    query_row = lax.broadcasted_iota(jnp.int32, (B, width), 1) & (B - 1)
    own_mask = key_row <= query_row

    def keys_of(d):
        if isinstance(d, int) and d == 0:
            return k_ref, v_ref
        return kv_win.at[d - 1, 0], kv_win.at[d - 1, 1]

    def key_span(d, i):
        if isinstance(i, int) and isinstance(d, int) and d == 0:
            return 0, i + 1
        if isinstance(i, int) and isinstance(d, int) and d == reach:
            return i, nb
        return 0, nb

    def biased(d, i, j, raw):
        offset = d * nb + i - j
        if isinstance(i, int) and offset == 0:
            return jnp.where(own_mask, raw, -jnp.inf), jnp.float32(0.0)
        if isinstance(i, int) and offset == 1:
            return jnp.where(own_mask, -jnp.inf, raw), jnp.float32(0.0)
        key_block = (me - d) * nb + j
        hits = jnp.int32(0)
        for n in range(listed_count):
            hits = hits | (docs_ref[i, n] == key_block).astype(jnp.int32)
        ok = (hits > 0) & (offset >= 2)
        return raw, jnp.where(ok, jnp.float32(0.0), jnp.float32(-jnp.inf))

    def raw_blocks(d, i):
        low, high = key_span(d, i)
        raw = dot_t(keys_of(d)[0][low * B : high * B, :], q_heads[i])
        return [
            biased(d, i, j, raw[(j - low) * B : (j - low + 1) * B]) for j in range(low, high)
        ]

    def score_step(d, i, fresh):
        low, high = key_span(d, i)
        blocks = raw_blocks(d, i)
        tops = [jnp.max(raw, axis=0, keepdims=True) * scale2 + bias for raw, bias in blocks]
        top = jnp.maximum(functools.reduce(jnp.maximum, tops), FLOOR)
        total = 0.0
        for j, (raw, bias) in enumerate(blocks):
            weight = jnp.exp2(raw * scale2 + (bias - top))
            total = total + jnp.sum(weight, axis=0, keepdims=True)
            probs[d, i, (low + j) * B : (low + j + 1) * B, :] = weight.astype(jnp.bfloat16)
        stats[d, i, 0:1, :] = top
        stats[d, i, 1:2, :] = total

    def delta_step(d, i, fresh):
        low, high = key_span(d, i)
        prob_grad = dot_t(keys_of(d)[1][low * B : high * B, :], g_heads[i])
        weight = probs[d, i, low * B : high * B, :].astype(jnp.float32)
        stats[d, i, 2:3, :] = jnp.sum(weight * prob_grad, axis=0, keepdims=True)

    def late_delta_step(d, i, fresh):
        low, high = key_span(d, i)
        prob_grad = dot_t(keys_of(d)[1][low * B : high * B, :], g_heads[i])
        weight = probs[d, i, low * B : high * B, :].astype(jnp.float32)
        total = jnp.sum(weight * prob_grad, axis=0, keepdims=True)
        stats[d, i, 2:3, :] = total
        done = jnp.logical_or(jnp.int32(d) == reach, jnp.int32(i) == nb - 1)
        stats[d, i, 3:4, :] = jnp.where(done, jnp.float32(1.0), stats[d, i, 1:2, :])

    def value_step(d, i, fresh):
        low, high = key_span(d, i)
        weight = probs[d, i, low * B : high * B, :].astype(jnp.float32)
        prob_half = (weight * stats[d, i, 1:2, :]).astype(jnp.bfloat16)
        probs[d, i, low * B : high * B, :] = prob_half
        term = dot_n(prob_half, g_heads[i])
        if fresh:
            kv_sum[d, 1, low * B : high * B, :] = term
        else:
            kv_sum[d, 1, low * B : high * B, :] += term

    def grad_step(d, i, fresh):
        low, high = key_span(d, i)
        keys = keys_of(d)[0][low * B : high * B, :]
        prob_grad = dot_t(keys_of(d)[1][low * B : high * B, :], g_heads[i])
        prob = probs[d, i, low * B : high * B, :].astype(jnp.float32)
        score_half = (prob * (prob_grad - delta[i, 0:1, :])).astype(jnp.bfloat16)
        term = dot_n(score_half, q_heads[i])
        if fresh:
            kv_sum[d, 0, low * B : high * B, :] = term
        else:
            kv_sum[d, 0, low * B : high * B, :] += term
        dq_sum[i] += dot_lt(keys, score_half)

    def over_blocks(d, step):
        if d == 0:
            for i in range(nb - 1, -1, -1):
                step(d, i, i == nb - 1)
            return
        step(d, 0, True)
        if d == reach:
            for i in range(1, nb):
                step(d, i, False)
            return

        def one(i, carry):
            step(d, i, False)
            return carry

        lax.fori_loop(1, nb, one, 0)

    def present(d, step, extra=None):
        @pl.when(me >= d if extra is None else (me >= d) & extra)
        def _():
            over_blocks(d, step)

    def arrive(d, c):
        @pl.when(me >= d)
        def _():
            forward(d - 1, c).wait_recv()

        if d < reach:

            @pl.when((me >= d) & has_next)
            def _():
                forward(d, c).start()

    def scaled(d, c):
        return kv_sum[d, c] * scale if c == 0 else kv_sum[d, c]

    def send_first(d, c):
        first = me >= d if d == reach else (me >= d) & jnp.logical_not(has_next)

        @pl.when(first)
        def _():
            ret_out[d - 1, c] = scaled(d, c).astype(jnp.bfloat16)
            backward(d, c).start()

    def send_on(d, c):
        @pl.when((me >= d) & has_next)
        def _():
            backward(d + 1, c).wait_recv()
            ret_out[d - 1, c] = (scaled(d, c) + ret_in[d, c].astype(jnp.float32)).astype(jnp.bfloat16)
            backward(d, c).start()

    present(0, score_step)
    present(0, delta_step)
    for d in range(1, reach + 1):
        arrive(d, 0)
        present(d, score_step)
        if d < reach:

            @pl.when(me > d)
            def _():
                forward(d - 1, 1).wait_recv()

                @pl.when(has_next)
                def _():
                    forward(d, 1).start()

                over_blocks(d, delta_step)

    for i in range(nb):
        tops = [stats[d, i, 0:1, :] for d in range(reach + 1)]
        top = functools.reduce(jnp.maximum, tops)
        parts = [jnp.exp2(t - top) for t in tops]
        total = functools.reduce(jnp.add, [parts[d] * stats[d, i, 1:2, :] for d in range(reach + 1)])
        inverse = 1.0 / total
        for d in range(reach + 1):
            stats[d, i, 1:2, :] = parts[d] * inverse
            stats[d, i, 3:4, :] = parts[d] * inverse

    top, second = nb - 1, nb - 2

    def over_near(i, step):
        step(0, i, i == top)

        def one(d, carry):
            step(d, i, i == top)
            return carry

        if reach > 1:
            lax.fori_loop(1, jnp.minimum(me, reach - 1) + 1, one, 0)

    def over_rest(d, step, count):
        @pl.when(me >= d)
        def _():
            if d in (0, reach):
                for i in range(count - 1, -1, -1):
                    step(d, i, False)
                return

            def one(i, carry):
                step(d, i, False)
                return carry

            lax.fori_loop(0, count, one, 0)

    def finish(i):
        part = slice(i * B, (i + 1) * B)
        turned = (dq_sum[i] * scale).T.astype(jnp.bfloat16)
        for h in range(heads):
            dq_ref[part, h * HEAD_WIDTH : (h + 1) * HEAD_WIDTH] = turned[h * B : (h + 1) * B]

        @pl.when(jnp.logical_not(has_next))
        def _():
            for c in range(2):
                own = kv_sum[0, c, part, :] * scale if c == 0 else kv_sum[0, c, part, :]
                dkv_now[part, c * HEAD_WIDTH : (c + 1) * HEAD_WIDTH] = own.astype(jnp.bfloat16)

    half_cols = cols // 2

    def term(owner, c, h, keep):
        span = pl.ds(pl.multiple_of(owner * cols + h * half_cols, half_cols), half_cols)
        part = slice(c * B, (c + 1) * B)
        value = dot_t(dq_ref[part, :], wq_ref[span, :])
        if keep:
            value = value + dot_t(dkv_now[part, :HEAD_WIDTH], wk_ref[span, :])
            value = value + dot_t(dkv_now[part, HEAD_WIDTH:], wv_ref[span, :])
        return value

    def to_pair(k, c, h):
        return pltpu.make_async_remote_copy(
            src_ref=pair_out.at[k, c, h],
            dst_ref=pair_in.at[k, c, h],
            send_sem=pair_send.at[k, c, h],
            recv_sem=pair_recv.at[k, c, h],
            device_id={"tp": partner},
            device_id_type=MESH_ID,
        )

    def to_far(k, c, h):
        return pltpu.make_async_remote_copy(
            src_ref=far_out.at[k - 1, c, h],
            dst_ref=far_in.at[k - 1, c, h],
            send_sem=far_send.at[k - 1, c, h],
            recv_sem=far_recv.at[k - 1, c, h],
            device_id={"tp": peer_of(k)},
            device_id_type=MESH_ID,
        )

    def both(step):
        @pl.when(has_next)
        def _():
            step(False)

        @pl.when(jnp.logical_not(has_next))
        def _():
            step(True)

    def give(k, c, h, keep):
        pair_out[k, c, h] = term(owner_of(k, False), c, h, keep).astype(jnp.bfloat16)
        to_pair(k, c, h).start()

    def take(k, c, h, keep):
        value = term(owner_of(k, True), c, h, keep)
        to_pair(k, c, h).wait_recv()
        value = value + pair_in[k, c, h].astype(jnp.float32)
        if k == 0:
            near_sum[c * B : (c + 1) * B, h * half_cols : (h + 1) * half_cols] = value
        else:
            far_out[k - 1, c, h] = value.astype(jnp.bfloat16)
            to_far(k, c, h).start()

    def far_terms(c):
        def step(keep):
            for k in range(1, pairs):
                for h in range(2):
                    give(k, c, h, keep)
                for h in range(2):
                    take(k, c, h, keep)

        both(step)

    def near_terms():
        def step(keep):
            order = [(c, h) for c in range(nb - 1, -1, -1) for h in range(2)]
            for n in range(len(order) + 2):
                if n < len(order):
                    give(0, *order[n], keep)
                if n >= 2:
                    take(0, *order[n - 2], keep)

        both(step)

    def gather(k, m, c):
        return pltpu.make_async_remote_copy(
            src_ref=dkv_all.at[c, :, slot(k, 0)] if m == 1 else dkv_all.at[c, :, slot(0, 0)],
            dst_ref=dkv_all.at[c, :, slot(k, m)],
            send_sem=gather_send.at[k, m, c],
            recv_sem=gather_recv.at[k, m, c],
            device_id={"tp": partner if m == 1 else peer_of(k)},
            device_id_type=MESH_ID,
        )

    def settle(c):
        @pl.when(has_next)
        def _():
            backward(1, c).wait_recv()
            dkv_all[c, :, 0:HEAD_WIDTH] = (scaled(0, c) + ret_in[0, c].astype(jnp.float32)).astype(jnp.bfloat16)
            for k in range(1, pairs):
                gather(k, 0, c).start()
            gather(0, 1, c).start()

    def add_terms(k, c):
        lanes = slice(2 * k * HEAD_WIDTH, (2 * k + 2) * HEAD_WIDTH)
        step_cols = min(256, cols)
        for n in range(0, cols, step_cols):
            near_sum[:, n : n + step_cols] += dot_t(dkv_all[c, :, lanes], kw_all[c, n : n + step_cols, lanes])

    def near_adds(c):
        gather(0, 1, c).wait_recv()
        add_terms(0, c)

    def far_passes(c):
        for k in range(1, pairs):
            gather(k, 0, c).wait_recv()
            gather(k, 1, c).start()

    def far_adds(c):
        for k in range(1, pairs):
            gather(k, 1, c).wait_recv()
            add_terms(k, c)

    present(reach, value_step)
    send_first(reach, 1)
    over_near(top, value_step)

    for d in range(1, reach + 1):

        @pl.when(me >= reach if d == reach else me == d)
        def _():
            forward(d - 1, 1).wait_recv()
            if d < reach:

                @pl.when(has_next)
                def _():
                    forward(d, 1).start()

            over_blocks(d, late_delta_step)

    for i in range(nb):
        delta[i, 0:1, :] = functools.reduce(
            jnp.add, [stats[d, i, 3:4, :] * stats[d, i, 2:3, :] for d in range(reach + 1)]
        )

    over_near(top, grad_step)

    @pl.when(me >= reach)
    def _():
        grad_step(reach, top, False)

    finish(top)
    for copy in whole:
        copy.wait()
    far_terms(top)

    if relayed:

        @pl.when(has_next)
        def _():
            for c in (1, 0):
                for k in range(1, pairs):
                    fetch(k, group, c).wait_recv()
                    relay(k, c).start()

    over_rest(reach, grad_step, top)
    send_first(reach, 0)
    if reach > 1:
        over_rest(reach - 1, value_step, top)
        send_first(reach - 1, 1)

    def rest_value(d, i, fresh):
        if isinstance(d, int):
            value_step(d, i, fresh)
        else:

            @pl.when(d < reach - 1)
            def _():
                value_step(d, i, fresh)

    over_near(second, rest_value)
    over_near(second, grad_step)
    finish(second)
    far_terms(second)
    if reach > 2:
        send_on(reach - 1, 1)
    for d in range(reach - 2, 0, -1):
        over_rest(d, value_step, second)
        send_first(d, 1)
    for d in range(reach - 1, 0, -1):
        over_rest(d, grad_step, second)
        send_first(d, 0)
    over_rest(0, value_step, second)
    over_rest(0, grad_step, second)
    for i in range(second - 1, -1, -1):
        finish(i)
        far_terms(i)
    for d in range(reach - 2, 1, -1):
        send_on(d, 1)
    for d in range(reach - 1, 1, -1):
        send_on(d, 0)
    near_terms()
    if reach > 1:
        send_on(1, 1)
        send_on(1, 0)
    settle(1)

    @pl.when(has_next)
    def _():
        for c in range(2):
            own_weights(c).wait()
            fetch(0, 1, c).wait_recv()
        near_adds(1)

    settle(0)

    @pl.when(has_next)
    def _():
        for k in range(1, pairs):
            for c in range(2):
                if relayed:
                    relay(k, c, True).wait_recv()
                else:
                    for m in range(2):
                        fetch(k, m, c).wait_recv()
        far_passes(1)
        near_adds(0)
        far_adds(1)
        far_passes(0)
        far_adds(0)

    near = list(range(nb - 1, -1, -1))
    for c in near:
        for h in range(2):
            part = (slice(c * B, (c + 1) * B), slice(h * half_cols, (h + 1) * half_cols))
            value = near_sum[part]
            for k in range(1, pairs):
                to_far(k, c, h).wait_recv()
                value = value + far_in[k - 1, c, h].astype(jnp.float32)
            out_ref[part] = value.astype(jnp.bfloat16)

    @pl.when(has_next)
    def _():
        for k, m in others:
            for c in range(2):
                gather(k, m, c).wait_send()
        for item in fetches:
            fetch(*item).wait_send()
        if relayed:
            for k in range(1, pairs):
                for c in range(2):
                    relay(k, c).wait_send()

    for c in near:
        for h in range(2):
            for k in range(pairs):
                to_pair(k, c, h).wait_send()
                if k > 0:
                    to_far(k, c, h).wait_send()

    for d in range(reach):

        @pl.when((me >= d) & has_next)
        def _():
            for c in range(2):
                forward(d, c).wait_send()

        @pl.when(me >= d + 1)
        def _():
            for c in range(2):
                backward(d + 1, c).wait_send()


def body(
    query,
    key_head_rows,
    value_head_rows,
    output_gradient,
    doc_blocks,
    w_query,
    key_weight,
    value_weight,
):
    shards = lax.axis_size("seq")
    places = lax.axis_size("tp")
    groups = lax.axis_size("groups")
    pairs = places // 2
    reach = min(8, shards - 1)
    rows, q_width = query.shape
    nb = rows // BLOCK_POSITIONS
    cols = w_query.shape[0] // places
    width = (q_width // HEAD_WIDTH) * BLOCK_POSITIONS
    half, full = jnp.bfloat16, jnp.float32
    vmem = pl.BlockSpec(memory_space=pltpu.VMEM)
    hbm = pl.BlockSpec(memory_space=pltpu.HBM)
    dma = pltpu.SemaphoreType.DMA
    buffers = [
        ((rows, q_width), half),
        ((rows, HEAD_WIDTH), half),
        ((rows, HEAD_WIDTH), half),
        ((rows, q_width), half),
        ((rows, q_width), half),
        ((rows, 2 * HEAD_WIDTH), half),
        ((2, rows, 2 * pairs * HEAD_WIDTH), half),
        ((2, cols, 2 * pairs * HEAD_WIDTH), half),
        (w_query.shape, half),
        (key_weight.shape, half),
        (value_weight.shape, half),
        ((rows, cols), full),
        ((pairs, nb, 2, rows // nb, cols // 2), half),
        ((pairs, nb, 2, rows // nb, cols // 2), half),
        ((pairs - 1, nb, 2, rows // nb, cols // 2), half),
        ((pairs - 1, nb, 2, rows // nb, cols // 2), half),
    ]
    later = [
        ((reach, 2, rows, HEAD_WIDTH), half),
        ((nb, width, HEAD_WIDTH), half),
        ((nb, width, HEAD_WIDTH), half),
        ((reach + 1, nb, 8, width), full),
        ((nb, 8, width), full),
        ((nb, HEAD_WIDTH, width), full),
        ((reach + 1, nb, rows, width), half),
        ((reach + 1, 2, rows, HEAD_WIDTH), full),
        ((reach, 2, rows, HEAD_WIDTH), half),
        ((reach, 2, rows, HEAD_WIDTH), half),
    ]
    used = sum(math.prod(shape) * jnp.dtype(kind).itemsize for shape, kind in buffers + later)
    limit = min(used + SPARE_MIB * 1024 * 1024, 60 * 1024 * 1024)
    return pl.pallas_call(
        functools.partial(attention_kernel, shards, reach, places, groups),
        out_shape=jax.ShapeDtypeStruct((rows, cols), half),
        in_specs=[hbm] * 8,
        out_specs=vmem,
        scratch_shapes=[pltpu.SMEM(doc_blocks.shape, doc_blocks.dtype)]
        + [pltpu.VMEM(*item) for item in buffers]
        + [
            dma((5,)),
            dma((3,)),
            dma((pairs, nb, 2)),
            dma((pairs, nb, 2)),
            dma((pairs - 1, nb, 2)),
            dma((pairs - 1, nb, 2)),
            dma((pairs, 2, 2)),
            dma((pairs, 2, 2)),
            dma((pairs, 2)),
            dma((pairs, 2)),
            dma((pairs, 2, 2)),
            dma((pairs, 2, 2)),
        ]
        + [pltpu.VMEM(*item) for item in later]
        + [
            dma((reach, 2)),
            dma((reach, 2)),
            dma((reach, 2)),
            dma((reach, 2)),
        ],
        compiler_params=pltpu.CompilerParams(
            collective_id=0, has_side_effects=True, vmem_limit_bytes=limit
        ),
        name="attention",
    )(
        pltpu.with_memory_space_constraint(query, pltpu.HBM),
        pltpu.with_memory_space_constraint(key_head_rows, pltpu.HBM),
        pltpu.with_memory_space_constraint(value_head_rows, pltpu.HBM),
        pltpu.with_memory_space_constraint(output_gradient, pltpu.HBM),
        pltpu.with_memory_space_constraint(doc_blocks, pltpu.HBM),
        pltpu.with_memory_space_constraint(w_query, pltpu.HBM),
        pltpu.with_memory_space_constraint(key_weight, pltpu.HBM),
        pltpu.with_memory_space_constraint(value_weight, pltpu.HBM),
    )


def solution(mesh):
    in_specs = (
        P(("groups", "seq"), "tp"),
        P(("groups", "seq"), "tp"),
        P(("groups", "seq"), "tp"),
        P(("groups", "seq"), "tp"),
        P(("groups", "seq"), None),
        P(None, "tp"),
        P(None, "tp"),
        P(None, "tp"),
    )
    out_specs = P(("groups", "seq"), "tp")
    return jax.shard_map(body, mesh=mesh, in_specs=in_specs, out_specs=out_specs, check_vma=False)
```

```python
import functools
import math

import jax
import jax.numpy as jnp
from jax import lax
from jax.experimental import pallas as pl
from jax.experimental.pallas import tpu as pltpu
from jax.sharding import PartitionSpec as P

HEAD_WIDTH = 128
BLOCK_POSITIONS = 128
MESH_ID = pl.DeviceIdType.MESH
SPARE_MIB = 12


def dot_t(a, b):
    return lax.dot_general(a, b, (((1,), (1,)), ((), ())), preferred_element_type=jnp.float32)


def dot_n(a, b):
    return lax.dot_general(a, b, (((1,), (0,)), ((), ())), preferred_element_type=jnp.float32)


def dot_lt(a, b):
    return lax.dot_general(a, b, (((0,), (0,)), ((), ())), preferred_element_type=jnp.float32)


FLOOR = -1e9


def attention_kernel(
    shards,
    reach,
    places,
    groups,
    q_hbm,
    k_hbm,
    v_hbm,
    g_hbm,
    docs_hbm,
    wq_hbm,
    wk_hbm,
    wv_hbm,
    out_ref,
    docs_ref,
    q_ref,
    k_ref,
    v_ref,
    g_ref,
    dq_ref,
    dkv_now,
    dkv_all,
    kw_all,
    wq_ref,
    wk_ref,
    wv_ref,
    near_sum,
    near_out,
    near_in,
    pair_out,
    pair_in,
    far_out,
    far_in,
    load_sem,
    weight_sem,
    near_send,
    near_recv,
    pair_send,
    pair_recv,
    far_send,
    far_recv,
    fetch_send,
    fetch_recv,
    relay_send,
    relay_recv,
    gather_send,
    gather_recv,
    kv_win,
    q_heads,
    g_heads,
    stats,
    delta,
    dq_sum,
    probs,
    kv_sum,
    ret_out,
    ret_in,
    send_sem,
    recv_sem,
    ret_send,
    ret_recv,
):
    B = BLOCK_POSITIONS
    rows = k_ref.shape[0]
    nb = rows // B
    heads = q_ref.shape[1] // HEAD_WIDTH
    listed_count = docs_ref.shape[1]
    me = lax.axis_index("seq")
    scale = HEAD_WIDTH ** -0.5
    scale2 = scale * math.log2(math.e)
    has_next = me + 1 < shards
    has_prev = me >= 1

    pairs = places // 2
    place = lax.axis_index("tp")
    my_pair = place // 2
    parity = place % 2
    partner = my_pair * 2 + 1 - parity
    cols = out_ref.shape[1]
    relayed = groups == 2
    group = lax.axis_index("groups")

    def peer_of(k):
        return lax.rem(my_pair + k, pairs) * 2 + parity

    def owner_of(k, mine):
        return lax.rem(my_pair + k, pairs) * 2 + (parity if mine else 1 - parity)

    loads = [
        pltpu.make_async_copy(src, dst, load_sem.at[n])
        for n, (src, dst) in enumerate(((k_hbm, k_ref), (q_hbm, q_ref), (v_hbm, v_ref), (g_hbm, g_ref), (docs_hbm, docs_ref)))
    ]
    for copy in loads:
        copy.start()

    barrier = pltpu.get_barrier_semaphore()
    others = [(k, m) for k in range(pairs) for m in range(2) if (k, m) != (0, 0)]
    for k, m in others:
        pl.semaphore_signal(barrier, inc=1, device_id={"tp": owner_of(k, m == 0)}, device_id_type=MESH_ID)
    if relayed:
        pl.semaphore_signal(barrier, inc=1, device_id={"groups": 1 - group}, device_id_type=MESH_ID)

    @pl.when(has_next)
    def _():
        pl.semaphore_signal(barrier, inc=1, device_id={"seq": me + 1}, device_id_type=MESH_ID)

    @pl.when(has_prev)
    def _():
        pl.semaphore_signal(barrier, inc=1, device_id={"seq": me - 1}, device_id_type=MESH_ID)

    greeted = places - 1 + (1 if relayed else 0)
    pl.semaphore_wait(barrier, has_next.astype(jnp.int32) + has_prev.astype(jnp.int32) + greeted)

    def forward(d, c):
        src = (k_hbm, v_hbm)[c] if d == 0 else kv_win.at[d - 1, c]
        return pltpu.make_async_remote_copy(
            src_ref=src,
            dst_ref=kv_win.at[d, c],
            send_sem=send_sem.at[d, c],
            recv_sem=recv_sem.at[d, c],
            device_id={"seq": jnp.minimum(me + 1, shards - 1)},
            device_id_type=MESH_ID,
        )

    def backward(d, c):
        return pltpu.make_async_remote_copy(
            src_ref=ret_out.at[d - 1, c],
            dst_ref=ret_in.at[d - 1, c],
            send_sem=ret_send.at[d - 1, c],
            recv_sem=ret_recv.at[d - 1, c],
            device_id={"seq": jnp.maximum(me - 1, 0)},
            device_id_type=MESH_ID,
        )

    def span_of(owner):
        return pl.ds(pl.multiple_of(owner * cols, cols), cols)

    def slot(k, m):
        lane = (2 * k + m) * HEAD_WIDTH
        return pl.ds(lane if isinstance(m, int) else pl.multiple_of(lane, HEAD_WIDTH), HEAD_WIDTH)

    def fetch(k, m, c):
        if isinstance(m, int):
            owner = owner_of(k, m == 0)
        else:
            owner = lax.rem(my_pair + k, pairs) * 2 + lax.rem(parity + m, 2)
        return pltpu.make_async_remote_copy(
            src_ref=(wk_hbm, wv_hbm)[c].at[span_of(owner)],
            dst_ref=kw_all.at[c, :, slot(k, m)],
            send_sem=fetch_send.at[k, m, c],
            recv_sem=fetch_recv.at[k, m, c],
            device_id={"tp": owner},
            device_id_type=MESH_ID,
        )

    def own_weights(c):
        return pltpu.make_async_copy(
            (wk_hbm, wv_hbm)[c].at[span_of(place)], kw_all.at[c, :, slot(0, 0)], fetch_recv.at[0, 0, c]
        )

    def relay(k, c, arriving=False):
        which = 1 - group if arriving else group
        return pltpu.make_async_remote_copy(
            src_ref=kw_all.at[c, :, slot(k, which)],
            dst_ref=kw_all.at[c, :, slot(k, which)],
            send_sem=relay_send.at[k, c],
            recv_sem=relay_recv.at[k, c],
            device_id={"groups": 1 - group},
            device_id_type=MESH_ID,
        )

    if relayed:
        fetches = [(0, 1, c) for c in range(2)] + [(k, group, c) for c in (1, 0) for k in range(1, pairs)]
    else:
        fetches = [(k, m, c) for k, m in others for c in range(2)]

    @pl.when(has_next)
    def _():
        forward(0, 0).start()

        @pl.when(me != 1)
        def _():
            forward(0, 1).start()

        for item in fetches:
            fetch(*item).start()
        for c in range(2):
            own_weights(c).start()

    whole = [
        pltpu.make_async_copy(wq_hbm, wq_ref, weight_sem.at[0]),
        pltpu.make_async_copy(wk_hbm, wk_ref, weight_sem.at[1]),
        pltpu.make_async_copy(wv_hbm, wv_ref, weight_sem.at[2]),
    ]
    for copy in whole:
        copy.start()

    width = heads * B
    for d in range(1, reach + 1):
        for i in range(nb):
            stats[d, i, 0:1, :] = jnp.full((1, width), FLOOR, jnp.float32)
            stats[d, i, 1:3, :] = jnp.zeros((2, width), jnp.float32)

    for i in range(nb):
        dq_sum[i] = jnp.zeros((HEAD_WIDTH, width), jnp.float32)

    @pl.when(me >= reach)
    def _():
        kv_sum[reach, 0] = jnp.zeros((rows, HEAD_WIDTH), jnp.float32)

    for copy in loads:
        copy.wait()
    for i in range(nb):
        for h in range(heads):
            q_heads[i, h * B : (h + 1) * B, :] = q_ref[i * B : (i + 1) * B, h * HEAD_WIDTH : (h + 1) * HEAD_WIDTH]
            g_heads[i, h * B : (h + 1) * B, :] = g_ref[i * B : (i + 1) * B, h * HEAD_WIDTH : (h + 1) * HEAD_WIDTH]
    key_row = lax.broadcasted_iota(jnp.int32, (B, width), 0)
    query_row = lax.broadcasted_iota(jnp.int32, (B, width), 1) & (B - 1)
    own_mask = key_row <= query_row

    def keys_of(d):
        if isinstance(d, int) and d == 0:
            return k_ref, v_ref
        return kv_win.at[d - 1, 0], kv_win.at[d - 1, 1]

    def key_span(d, i):
        if isinstance(i, int) and isinstance(d, int) and d == 0:
            return 0, i + 1
        if isinstance(i, int) and isinstance(d, int) and d == reach:
            return i, nb
        return 0, nb

    def biased(d, i, j, raw):
        offset = d * nb + i - j
        if isinstance(i, int) and offset == 0:
            return jnp.where(own_mask, raw, -jnp.inf), jnp.float32(0.0)
        if isinstance(i, int) and offset == 1:
            return jnp.where(own_mask, -jnp.inf, raw), jnp.float32(0.0)
        key_block = (me - d) * nb + j
        hits = jnp.int32(0)
        for n in range(listed_count):
            hits = hits | (docs_ref[i, n] == key_block).astype(jnp.int32)
        ok = (hits > 0) & (offset >= 2)
        return raw, jnp.where(ok, jnp.float32(0.0), jnp.float32(-jnp.inf))

    def raw_blocks(d, i):
        low, high = key_span(d, i)
        raw = dot_t(keys_of(d)[0][low * B : high * B, :], q_heads[i])
        return [
            biased(d, i, j, raw[(j - low) * B : (j - low + 1) * B]) for j in range(low, high)
        ]

    def score_step(d, i, fresh):
        low, high = key_span(d, i)
        blocks = raw_blocks(d, i)
        tops = [jnp.max(raw, axis=0, keepdims=True) * scale2 + bias for raw, bias in blocks]
        top = jnp.maximum(functools.reduce(jnp.maximum, tops), FLOOR)
        total = 0.0
        for j, (raw, bias) in enumerate(blocks):
            weight = jnp.exp2(raw * scale2 + (bias - top))
            total = total + jnp.sum(weight, axis=0, keepdims=True)
            probs[d, i, (low + j) * B : (low + j + 1) * B, :] = weight.astype(jnp.bfloat16)
        stats[d, i, 0:1, :] = top
        stats[d, i, 1:2, :] = total

    def delta_step(d, i, fresh):
        low, high = key_span(d, i)
        prob_grad = dot_t(keys_of(d)[1][low * B : high * B, :], g_heads[i])
        weight = probs[d, i, low * B : high * B, :].astype(jnp.float32)
        stats[d, i, 2:3, :] = jnp.sum(weight * prob_grad, axis=0, keepdims=True)

    def scaled_delta_step(whole_from):
        def step(d, i, fresh):
            delta_step(d, i, fresh)
            done = jnp.logical_or(jnp.int32(d) >= whole_from, jnp.int32(i) == nb - 1)
            stats[d, i, 3:4, :] = jnp.where(done, jnp.float32(1.0), stats[d, i, 1:2, :])

        return step

    def value_step(d, i, fresh):
        low, high = key_span(d, i)
        weight = probs[d, i, low * B : high * B, :].astype(jnp.float32)
        prob_half = (weight * stats[d, i, 1:2, :]).astype(jnp.bfloat16)
        probs[d, i, low * B : high * B, :] = prob_half
        term = dot_n(prob_half, g_heads[i])
        if fresh:
            kv_sum[d, 1, low * B : high * B, :] = term
        else:
            kv_sum[d, 1, low * B : high * B, :] += term

    def grad_step(d, i, fresh):
        low, high = key_span(d, i)
        keys = keys_of(d)[0][low * B : high * B, :]
        prob_grad = dot_t(keys_of(d)[1][low * B : high * B, :], g_heads[i])
        prob = probs[d, i, low * B : high * B, :].astype(jnp.float32)
        score_half = (prob * (prob_grad - delta[i, 0:1, :])).astype(jnp.bfloat16)
        term = dot_n(score_half, q_heads[i])
        if fresh:
            kv_sum[d, 0, low * B : high * B, :] = term
        else:
            kv_sum[d, 0, low * B : high * B, :] += term
        dq_sum[i] += dot_lt(keys, score_half)

    def over_blocks(d, step):
        if d == 0:
            for i in range(nb - 1, -1, -1):
                step(d, i, i == nb - 1)
            return
        step(d, 0, True)
        if d == reach:
            for i in range(1, nb):
                step(d, i, False)
            return

        def one(i, carry):
            step(d, i, False)
            return carry

        lax.fori_loop(1, nb, one, 0)

    def present(d, step, extra=None):
        @pl.when(me >= d if extra is None else (me >= d) & extra)
        def _():
            over_blocks(d, step)

    def arrive(d, c, checked=True):
        there = me >= d if checked else True

        @pl.when(there)
        def _():
            forward(d - 1, c).wait_recv()

        if d < reach:

            @pl.when(there & has_next)
            def _():
                forward(d, c).start()

        if d == 1 and c == 0:

            @pl.when((me == 1) & has_next)
            def _():
                forward(0, 1).start()

    def take_values(d, step):
        arrive(d, 1, False)
        over_blocks(d, step)

    def scaled(d, c):
        return kv_sum[d, c] * scale if c == 0 else kv_sum[d, c]

    def send_first(d, c):
        first = me >= d if d == reach else (me >= d) & jnp.logical_not(has_next)

        @pl.when(first)
        def _():
            ret_out[d - 1, c] = scaled(d, c).astype(jnp.bfloat16)
            backward(d, c).start()

    def send_on(d, c, extra=None):
        @pl.when((me >= d if extra is None else extra) & has_next)
        def _():
            backward(d + 1, c).wait_recv()
            ret_out[d - 1, c] = (scaled(d, c) + ret_in[d, c].astype(jnp.float32)).astype(jnp.bfloat16)
            backward(d, c).start()

    present(0, score_step)
    present(0, delta_step)
    for d in range(1, reach + 1):
        arrive(d, 0)
        present(d, score_step)
        if d < reach:

            @pl.when(me > d + 1)
            def _():
                take_values(d, delta_step)

    for i in range(nb):
        tops = [stats[d, i, 0:1, :] for d in range(reach + 1)]
        top = functools.reduce(jnp.maximum, tops)
        parts = [jnp.exp2(t - top) for t in tops]
        total = functools.reduce(jnp.add, [parts[d] * stats[d, i, 1:2, :] for d in range(reach + 1)])
        inverse = 1.0 / total
        for d in range(reach + 1):
            stats[d, i, 1:2, :] = parts[d] * inverse
            stats[d, i, 3:4, :] = parts[d] * inverse

    top, second = nb - 1, nb - 2

    def over_near(i, step):
        step(0, i, i == top)

        def one(d, carry):
            step(d, i, i == top)
            return carry

        if reach > 1:
            lax.fori_loop(1, jnp.minimum(me, reach - 1) + 1, one, 0)

    def rest_value(d, i, fresh):
        if isinstance(d, int):
            value_step(d, i, fresh)
        else:

            @pl.when(d < reach - 1)
            def _():
                value_step(d, i, fresh)

    def rest_blocks(d, step, count):
        if d in (0, reach):
            for i in range(count - 1, -1, -1):
                step(d, i, False)
            return

        def one(i, carry):
            step(d, i, False)
            return carry

        lax.fori_loop(0, count, one, 0)

    def over_rest(d, step, count):
        @pl.when(me >= d)
        def _():
            rest_blocks(d, step, count)

    def finish(i):
        part = slice(i * B, (i + 1) * B)
        turned = (dq_sum[i] * scale).T.astype(jnp.bfloat16)
        for h in range(heads):
            dq_ref[part, h * HEAD_WIDTH : (h + 1) * HEAD_WIDTH] = turned[h * B : (h + 1) * B]

        @pl.when(jnp.logical_not(has_next))
        def _():
            for c in range(2):
                own = kv_sum[0, c, part, :] * scale if c == 0 else kv_sum[0, c, part, :]
                dkv_now[part, c * HEAD_WIDTH : (c + 1) * HEAD_WIDTH] = own.astype(jnp.bfloat16)

    half_cols = cols // 2
    piece = math.gcd(cols, 256)
    hold = me + 2 == shards

    def term(owner, part, first, count, keep):
        span = pl.ds(pl.multiple_of(owner * cols + first, count), count)
        value = dot_t(dq_ref[part, :], wq_ref[span, :])
        if keep:
            value = value + dot_t(dkv_now[part, :HEAD_WIDTH], wk_ref[span, :])
            value = value + dot_t(dkv_now[part, HEAD_WIDTH:], wv_ref[span, :])
        return value

    def to_pair(k, c, h):
        return pltpu.make_async_remote_copy(
            src_ref=pair_out.at[k - 1, c, h],
            dst_ref=pair_in.at[k - 1, c, h],
            send_sem=pair_send.at[k - 1, c, h],
            recv_sem=pair_recv.at[k - 1, c, h],
            device_id={"tp": partner},
            device_id_type=MESH_ID,
        )

    def to_far(k, c, h):
        return pltpu.make_async_remote_copy(
            src_ref=far_out.at[k - 1, c, h],
            dst_ref=far_in.at[k - 1, c, h],
            send_sem=far_send.at[k - 1, c, h],
            recv_sem=far_recv.at[k - 1, c, h],
            device_id={"tp": peer_of(k)},
            device_id_type=MESH_ID,
        )

    def to_near(n):
        return pltpu.make_async_remote_copy(
            src_ref=near_out.at[n],
            dst_ref=near_in.at[n],
            send_sem=near_send.at[n],
            recv_sem=near_recv.at[n],
            device_id={"tp": partner},
            device_id_type=MESH_ID,
        )

    def both(step):
        @pl.when(has_next)
        def _():
            step(False)

        @pl.when(jnp.logical_not(has_next))
        def _():
            step(True)

    def far_terms(low, count):
        part = slice(low * B, (low + count) * B)

        def step(keep):
            for k in range(1, pairs):
                for h in range(2):
                    value = term(owner_of(k, False), part, h * half_cols, half_cols, keep).astype(jnp.bfloat16)
                    for n in range(count - 1, -1, -1):
                        pair_out[k - 1, low + n, h] = value[n * B : (n + 1) * B]
                        to_pair(k, low + n, h).start()
                for h in range(2):
                    value = term(owner_of(k, True), part, h * half_cols, half_cols, keep)
                    for n in range(count - 1, -1, -1):
                        c = low + n
                        to_pair(k, c, h).wait_recv()
                        total = value[n * B : (n + 1) * B] + pair_in[k - 1, c, h].astype(jnp.float32)
                        far_out[k - 1, c, h] = total.astype(jnp.bfloat16)
                        if keep or (c, h) != (0, 1):
                            to_far(k, c, h).start()
                        else:

                            @pl.when(jnp.logical_not(hold))
                            def _():
                                to_far(k, c, h).start()

        both(step)

    def near_terms():
        def step(keep):
            part = slice(0, rows)
            count = cols // piece
            for n in range(count + 2):
                if n < count:
                    near_out[n] = term(partner, part, n * piece, piece, keep).astype(jnp.bfloat16)
                    to_near(n).start()
                if n >= 2:
                    value = term(place, part, (n - 2) * piece, piece, keep)
                    to_near(n - 2).wait_recv()
                    near_sum[:, (n - 2) * piece : (n - 1) * piece] = value + near_in[n - 2].astype(jnp.float32)

        both(step)

    def gather(k, m, c):
        return pltpu.make_async_remote_copy(
            src_ref=dkv_all.at[c, :, slot(k, 0)] if m == 1 else dkv_all.at[c, :, slot(0, 0)],
            dst_ref=dkv_all.at[c, :, slot(k, m)],
            send_sem=gather_send.at[k, m, c],
            recv_sem=gather_recv.at[k, m, c],
            device_id={"tp": partner if m == 1 else peer_of(k)},
            device_id_type=MESH_ID,
        )

    def settle(c):
        @pl.when(has_next)
        def _():
            backward(1, c).wait_recv()
            dkv_all[c, :, 0:HEAD_WIDTH] = (scaled(0, c) + ret_in[0, c].astype(jnp.float32)).astype(jnp.bfloat16)
            for k in range(1, pairs):
                gather(k, 0, c).start()
            gather(0, 1, c).start()

    def add_terms(k, c):
        lanes = slice(2 * k * HEAD_WIDTH, (2 * k + 2) * HEAD_WIDTH)
        step_cols = min(256, cols)
        for n in range(0, cols, step_cols):
            near_sum[:, n : n + step_cols] += dot_t(dkv_all[c, :, lanes], kw_all[c, n : n + step_cols, lanes])

    def near_adds(c):
        gather(0, 1, c).wait_recv()
        add_terms(0, c)

    def far_passes(c):
        for k in range(1, pairs):
            gather(k, 0, c).wait_recv()
            gather(k, 1, c).start()

    def far_adds(c):
        for k in range(1, pairs):
            gather(k, 1, c).wait_recv()
            add_terms(k, c)

    present(reach, value_step)
    send_first(reach, 1)
    over_near(top, value_step)

    for d in range(1, reach):

        @pl.when(me == d + 1)
        def _():
            take_values(d, scaled_delta_step(reach))

    late_step = scaled_delta_step(reach)
    for d in range(1, reach + 1):

        @pl.when(me >= reach if d == reach else me == d)
        def _():
            arrive(d, 1, False)
            late_step(d, top, False)

    def sum_delta(i):
        delta[i, 0:1, :] = functools.reduce(
            jnp.add, [stats[d, i, 3:4, :] * stats[d, i, 2:3, :] for d in range(reach + 1)]
        )

    sum_delta(top)
    over_near(top, grad_step)

    @pl.when(me >= reach)
    def _():
        grad_step(reach, top, False)

    finish(top)
    for copy in whole:
        copy.wait()
    far_terms(top, 1)

    if relayed:

        @pl.when(has_next)
        def _():
            for c in (1, 0):
                for k in range(1, pairs):
                    fetch(k, group, c).wait_recv()
                    relay(k, c).start()

    for d in range(1, reach + 1):

        @pl.when(me >= reach if d == reach else me == d)
        def _():
            rest_blocks(d, late_step, top)

    for i in range(top):
        sum_delta(i)
    over_rest(reach, grad_step, top)
    send_first(reach, 0)
    if reach > 1:
        over_rest(reach - 1, value_step, top)
        send_first(reach - 1, 1)
    over_near(second, rest_value)
    over_near(second, grad_step)
    finish(second)
    far_terms(second, 1)
    for d in range(reach - 2, 0, -1):
        over_rest(d, value_step, second)
        send_first(d, 1)
    over_rest(0, value_step, second)
    for d in range(reach - 1, 1, -1):
        send_on(d, 1)
    for d in range(reach - 1, 0, -1):
        over_rest(d, grad_step, second)
        send_first(d, 0)
    over_rest(0, grad_step, second)
    for i in range(second):
        finish(i)
    far_terms(0, second)
    for d in range(reach - 1, 1, -1):
        send_on(d, 0)
    near_terms()
    if reach > 1:
        send_on(1, 1)
        send_on(1, 0, me == 1)
    settle(1)
    if reach > 1:
        send_on(1, 0, me >= 2)

    @pl.when(has_next)
    def _():
        for c in range(2):
            own_weights(c).wait()
            fetch(0, 1, c).wait_recv()
        near_adds(1)

    settle(0)

    @pl.when(has_next)
    def _():
        @pl.when(hold)
        def _():
            for k in range(1, pairs):
                to_far(k, 0, 1).start()

        for k in range(1, pairs):
            for c in range(2):
                if relayed:
                    relay(k, c, True).wait_recv()
                else:
                    for m in range(2):
                        fetch(k, m, c).wait_recv()
        far_passes(1)
        near_adds(0)
        far_adds(1)
        far_passes(0)
        far_adds(0)

    near = list(range(nb - 1, -1, -1))
    for c in near:
        for h in range(2):
            part = (slice(c * B, (c + 1) * B), slice(h * half_cols, (h + 1) * half_cols))
            value = near_sum[part]
            for k in range(1, pairs):
                to_far(k, c, h).wait_recv()
                value = value + far_in[k - 1, c, h].astype(jnp.float32)
            out_ref[part] = value.astype(jnp.bfloat16)

    @pl.when(has_next)
    def _():
        for k, m in others:
            for c in range(2):
                gather(k, m, c).wait_send()
        for item in fetches:
            fetch(*item).wait_send()
        if relayed:
            for k in range(1, pairs):
                for c in range(2):
                    relay(k, c).wait_send()

    for c in near:
        for h in range(2):
            for k in range(1, pairs):
                to_pair(k, c, h).wait_send()
                to_far(k, c, h).wait_send()
    for n in range(cols // piece):
        to_near(n).wait_send()

    for d in range(reach):

        @pl.when((me >= d) & has_next)
        def _():
            for c in range(2):
                forward(d, c).wait_send()

        @pl.when(me >= d + 1)
        def _():
            for c in range(2):
                backward(d + 1, c).wait_send()


def body(
    query,
    key_head_rows,
    value_head_rows,
    output_gradient,
    doc_blocks,
    w_query,
    key_weight,
    value_weight,
):
    shards = lax.axis_size("seq")
    places = lax.axis_size("tp")
    groups = lax.axis_size("groups")
    pairs = places // 2
    reach = min(8, shards - 1)
    rows, q_width = query.shape
    nb = rows // BLOCK_POSITIONS
    cols = w_query.shape[0] // places
    width = (q_width // HEAD_WIDTH) * BLOCK_POSITIONS
    half, full = jnp.bfloat16, jnp.float32
    vmem = pl.BlockSpec(memory_space=pltpu.VMEM)
    hbm = pl.BlockSpec(memory_space=pltpu.HBM)
    dma = pltpu.SemaphoreType.DMA
    buffers = [
        ((rows, q_width), half),
        ((rows, HEAD_WIDTH), half),
        ((rows, HEAD_WIDTH), half),
        ((rows, q_width), half),
        ((rows, q_width), half),
        ((rows, 2 * HEAD_WIDTH), half),
        ((2, rows, 2 * pairs * HEAD_WIDTH), half),
        ((2, cols, 2 * pairs * HEAD_WIDTH), half),
        (w_query.shape, half),
        (key_weight.shape, half),
        (value_weight.shape, half),
        ((rows, cols), full),
        ((cols // math.gcd(cols, 256), rows, math.gcd(cols, 256)), half),
        ((cols // math.gcd(cols, 256), rows, math.gcd(cols, 256)), half),
        ((pairs - 1, nb, 2, rows // nb, cols // 2), half),
        ((pairs - 1, nb, 2, rows // nb, cols // 2), half),
        ((pairs - 1, nb, 2, rows // nb, cols // 2), half),
        ((pairs - 1, nb, 2, rows // nb, cols // 2), half),
    ]
    later = [
        ((reach, 2, rows, HEAD_WIDTH), half),
        ((nb, width, HEAD_WIDTH), half),
        ((nb, width, HEAD_WIDTH), half),
        ((reach + 1, nb, 8, width), full),
        ((nb, 8, width), full),
        ((nb, HEAD_WIDTH, width), full),
        ((reach + 1, nb, rows, width), half),
        ((reach + 1, 2, rows, HEAD_WIDTH), full),
        ((reach, 2, rows, HEAD_WIDTH), half),
        ((reach, 2, rows, HEAD_WIDTH), half),
    ]
    used = sum(math.prod(shape) * jnp.dtype(kind).itemsize for shape, kind in buffers + later)
    limit = min(used + SPARE_MIB * 1024 * 1024, 60 * 1024 * 1024)
    return pl.pallas_call(
        functools.partial(attention_kernel, shards, reach, places, groups),
        out_shape=jax.ShapeDtypeStruct((rows, cols), half),
        in_specs=[hbm] * 8,
        out_specs=vmem,
        scratch_shapes=[pltpu.SMEM(doc_blocks.shape, doc_blocks.dtype)]
        + [pltpu.VMEM(*item) for item in buffers]
        + [
            dma((5,)),
            dma((3,)),
            dma((cols // math.gcd(cols, 256),)),
            dma((cols // math.gcd(cols, 256),)),
            dma((pairs - 1, nb, 2)),
            dma((pairs - 1, nb, 2)),
            dma((pairs - 1, nb, 2)),
            dma((pairs - 1, nb, 2)),
            dma((pairs, 2, 2)),
            dma((pairs, 2, 2)),
            dma((pairs, 2)),
            dma((pairs, 2)),
            dma((pairs, 2, 2)),
            dma((pairs, 2, 2)),
        ]
        + [pltpu.VMEM(*item) for item in later]
        + [
            dma((reach, 2)),
            dma((reach, 2)),
            dma((reach, 2)),
            dma((reach, 2)),
        ],
        compiler_params=pltpu.CompilerParams(
            collective_id=0, has_side_effects=True, vmem_limit_bytes=limit
        ),
        name="attention",
    )(
        pltpu.with_memory_space_constraint(query, pltpu.HBM),
        pltpu.with_memory_space_constraint(key_head_rows, pltpu.HBM),
        pltpu.with_memory_space_constraint(value_head_rows, pltpu.HBM),
        pltpu.with_memory_space_constraint(output_gradient, pltpu.HBM),
        pltpu.with_memory_space_constraint(doc_blocks, pltpu.HBM),
        pltpu.with_memory_space_constraint(w_query, pltpu.HBM),
        pltpu.with_memory_space_constraint(key_weight, pltpu.HBM),
        pltpu.with_memory_space_constraint(value_weight, pltpu.HBM),
    )


def solution(mesh):
    in_specs = (
        P(("groups", "seq"), "tp"),
        P(("groups", "seq"), "tp"),
        P(("groups", "seq"), "tp"),
        P(("groups", "seq"), "tp"),
        P(("groups", "seq"), None),
        P(None, "tp"),
        P(None, "tp"),
        P(None, "tp"),
    )
    out_specs = P(("groups", "seq"), "tp")
    return jax.shard_map(body, mesh=mesh, in_specs=in_specs, out_specs=out_specs, check_vma=False)
```

```python
import functools
import math

import jax
import jax.numpy as jnp
from jax import lax
from jax.experimental import pallas as pl
from jax.experimental.pallas import tpu as pltpu
from jax.sharding import PartitionSpec as P

HEAD_WIDTH = 128
BLOCK_POSITIONS = 128
MESH_ID = pl.DeviceIdType.MESH
SPARE_MIB = 12


def dot_t(a, b):
    return lax.dot_general(a, b, (((1,), (1,)), ((), ())), preferred_element_type=jnp.float32)


def dot_n(a, b):
    return lax.dot_general(a, b, (((1,), (0,)), ((), ())), preferred_element_type=jnp.float32)


def dot_lt(a, b):
    return lax.dot_general(a, b, (((0,), (0,)), ((), ())), preferred_element_type=jnp.float32)


FLOOR = -1e9


def attention_kernel(
    shards,
    reach,
    places,
    groups,
    q_hbm,
    k_hbm,
    v_hbm,
    g_hbm,
    docs_hbm,
    wq_hbm,
    wk_hbm,
    wv_hbm,
    out_ref,
    docs_ref,
    q_ref,
    k_ref,
    v_ref,
    g_ref,
    dq_ref,
    turned_ref,
    dkv_all,
    kw_all,
    wq_ref,
    wk_ref,
    wv_ref,
    near_sum,
    near_out,
    near_in,
    pair_out,
    pair_in,
    far_out,
    far_in,
    load_sem,
    weight_sem,
    near_send,
    near_recv,
    pair_send,
    pair_recv,
    far_send,
    far_recv,
    fetch_send,
    fetch_recv,
    relay_send,
    relay_recv,
    gather_send,
    gather_recv,
    kv_win,
    q_heads,
    g_heads,
    stats,
    delta,
    dq_sum,
    probs,
    kv_sum,
    ret_out,
    ret_in,
    send_sem,
    recv_sem,
    last_send,
    last_recv,
    ret_send,
    ret_recv,
):
    B = BLOCK_POSITIONS
    rows = k_ref.shape[0]
    nb = rows // B
    heads = q_ref.shape[1] // HEAD_WIDTH
    lead = q_ref.shape[1]
    listed_count = docs_ref.shape[1]
    me = lax.axis_index("seq")
    scale = HEAD_WIDTH ** -0.5
    scale2 = scale * math.log2(math.e)
    has_next = me + 1 < shards
    has_prev = me >= 1

    pairs = places // 2
    place = lax.axis_index("tp")
    my_pair = place // 2
    parity = place % 2
    partner = my_pair * 2 + 1 - parity
    cols = out_ref.shape[1]
    relayed = groups == 2
    group = lax.axis_index("groups")

    def peer_of(k):
        return lax.rem(my_pair + k, pairs) * 2 + parity

    def owner_of(k, mine):
        return lax.rem(my_pair + k, pairs) * 2 + (parity if mine else 1 - parity)

    loads = [
        pltpu.make_async_copy(src, dst, load_sem.at[n])
        for n, (src, dst) in enumerate(((k_hbm, k_ref), (q_hbm, q_ref), (v_hbm, v_ref), (g_hbm, g_ref), (docs_hbm, docs_ref)))
    ]
    whole = [
        pltpu.make_async_copy(wq_hbm, wq_ref, weight_sem.at[0]),
        pltpu.make_async_copy(wk_hbm, wk_ref, weight_sem.at[1]),
        pltpu.make_async_copy(wv_hbm, wv_ref, weight_sem.at[2]),
    ]
    for copy in loads + whole:
        copy.start()

    barrier = pltpu.get_barrier_semaphore()
    others = [(k, m) for k in range(pairs) for m in range(2) if (k, m) != (0, 0)]
    for k, m in others:
        pl.semaphore_signal(barrier, inc=1, device_id={"tp": owner_of(k, m == 0)}, device_id_type=MESH_ID)
    if relayed:
        pl.semaphore_signal(barrier, inc=1, device_id={"groups": 1 - group}, device_id_type=MESH_ID)

    @pl.when(has_next)
    def _():
        pl.semaphore_signal(barrier, inc=1, device_id={"seq": me + 1}, device_id_type=MESH_ID)

    @pl.when(has_prev)
    def _():
        pl.semaphore_signal(barrier, inc=1, device_id={"seq": me - 1}, device_id_type=MESH_ID)

    greeted = places - 1 + (1 if relayed else 0)
    pl.semaphore_wait(barrier, has_next.astype(jnp.int32) + has_prev.astype(jnp.int32) + greeted)

    def forward(d, c):
        src = (k_hbm, v_hbm)[c] if d == 0 else kv_win.at[d - 1, c]
        return pltpu.make_async_remote_copy(
            src_ref=src,
            dst_ref=kv_win.at[d, c],
            send_sem=send_sem.at[d, c],
            recv_sem=recv_sem.at[d, c],
            device_id={"seq": jnp.minimum(me + 1, shards - 1)},
            device_id_type=MESH_ID,
        )

    def last_hop(n):
        span = pl.ds(rows - B, B) if n == 0 else pl.ds(0, rows - B)
        return pltpu.make_async_remote_copy(
            src_ref=(v_hbm if reach == 1 else kv_win.at[reach - 2, 1]).at[span],
            dst_ref=kv_win.at[reach - 1, 1, span],
            send_sem=last_send.at[n],
            recv_sem=last_recv.at[n],
            device_id={"seq": jnp.minimum(me + 1, shards - 1)},
            device_id_type=MESH_ID,
        )

    def backward(d, c):
        return pltpu.make_async_remote_copy(
            src_ref=ret_out.at[d - 1, c],
            dst_ref=ret_in.at[d - 1, c],
            send_sem=ret_send.at[d - 1, c],
            recv_sem=ret_recv.at[d - 1, c],
            device_id={"seq": jnp.maximum(me - 1, 0)},
            device_id_type=MESH_ID,
        )

    def span_of(owner):
        return pl.ds(pl.multiple_of(owner * cols, cols), cols)

    def slot(k, m):
        lane = (2 * k + m) * HEAD_WIDTH
        return pl.ds(lane if isinstance(m, int) else pl.multiple_of(lane, HEAD_WIDTH), HEAD_WIDTH)

    def fetch(k, m, c):
        if isinstance(m, int):
            owner = owner_of(k, m == 0)
        else:
            owner = lax.rem(my_pair + k, pairs) * 2 + lax.rem(parity + m, 2)
        return pltpu.make_async_remote_copy(
            src_ref=(wk_hbm, wv_hbm)[c].at[span_of(owner)],
            dst_ref=kw_all.at[c, :, slot(k, m)],
            send_sem=fetch_send.at[k, m, c],
            recv_sem=fetch_recv.at[k, m, c],
            device_id={"tp": owner},
            device_id_type=MESH_ID,
        )

    def own_weights(c):
        return pltpu.make_async_copy(
            (wk_hbm, wv_hbm)[c].at[span_of(place)], kw_all.at[c, :, slot(0, 0)], fetch_recv.at[0, 0, c]
        )

    def relay(k, c, arriving=False):
        which = 1 - group if arriving else group
        return pltpu.make_async_remote_copy(
            src_ref=kw_all.at[c, :, slot(k, which)],
            dst_ref=kw_all.at[c, :, slot(k, which)],
            send_sem=relay_send.at[k, c],
            recv_sem=relay_recv.at[k, c],
            device_id={"groups": 1 - group},
            device_id_type=MESH_ID,
        )

    if relayed:
        fetches = [(0, 1, c) for c in range(2)] + [(k, group, c) for c in (1, 0) for k in range(1, pairs)]
    else:
        fetches = [(k, m, c) for k, m in others for c in range(2)]

    @pl.when(has_next)
    def _():
        forward(0, 0).start()

        @pl.when(me != 1)
        def _():
            forward(0, 1).start()

        for item in fetches:
            fetch(*item).start()
        for c in range(2):
            own_weights(c).start()

    width = heads * B
    for d in range(1, reach + 1):
        for i in range(nb):
            stats[d, i, 0:1, :] = jnp.full((1, width), FLOOR, jnp.float32)
            stats[d, i, 1:3, :] = jnp.zeros((2, width), jnp.float32)

    for i in range(nb):
        dq_sum[i] = jnp.zeros((HEAD_WIDTH, width), jnp.float32)

    @pl.when(me >= reach)
    def _():
        kv_sum[reach, 0] = jnp.zeros((rows, HEAD_WIDTH), jnp.float32)

    for copy in loads:
        copy.wait()
    for i in range(nb):
        for h in range(heads):
            q_heads[i, h * B : (h + 1) * B, :] = q_ref[i * B : (i + 1) * B, h * HEAD_WIDTH : (h + 1) * HEAD_WIDTH]
            g_heads[i, h * B : (h + 1) * B, :] = g_ref[i * B : (i + 1) * B, h * HEAD_WIDTH : (h + 1) * HEAD_WIDTH]
    key_row = lax.broadcasted_iota(jnp.int32, (B, width), 0)
    query_row = lax.broadcasted_iota(jnp.int32, (B, width), 1) & (B - 1)
    own_mask = key_row <= query_row

    def keys_of(d):
        if isinstance(d, int) and d == 0:
            return k_ref, v_ref
        return kv_win.at[d - 1, 0], kv_win.at[d - 1, 1]

    def key_span(d, i):
        if isinstance(i, int) and isinstance(d, int) and d == 0:
            return 0, i + 1
        if isinstance(i, int) and isinstance(d, int) and d == reach:
            return i, nb
        return 0, nb

    def biased(d, i, j, raw):
        offset = d * nb + i - j
        if isinstance(i, int) and offset == 0:
            return jnp.where(own_mask, raw, -jnp.inf), jnp.float32(0.0)
        if isinstance(i, int) and offset == 1:
            return jnp.where(own_mask, -jnp.inf, raw), jnp.float32(0.0)
        key_block = (me - d) * nb + j
        hits = jnp.int32(0)
        for n in range(listed_count):
            hits = hits | (docs_ref[i, n] == key_block).astype(jnp.int32)
        ok = (hits > 0) & (offset >= 2)
        return raw, jnp.where(ok, jnp.float32(0.0), jnp.float32(-jnp.inf))

    def raw_blocks(d, i):
        low, high = key_span(d, i)
        raw = dot_t(keys_of(d)[0][low * B : high * B, :], q_heads[i])
        return [
            biased(d, i, j, raw[(j - low) * B : (j - low + 1) * B]) for j in range(low, high)
        ]

    def score_step(d, i, fresh):
        low, high = key_span(d, i)
        blocks = raw_blocks(d, i)
        tops = [jnp.max(raw, axis=0, keepdims=True) * scale2 + bias for raw, bias in blocks]
        top = jnp.maximum(functools.reduce(jnp.maximum, tops), FLOOR)
        total = 0.0
        for j, (raw, bias) in enumerate(blocks):
            weight = jnp.exp2(raw * scale2 + (bias - top))
            total = total + jnp.sum(weight, axis=0, keepdims=True)
            probs[d, i, (low + j) * B : (low + j + 1) * B, :] = weight.astype(jnp.bfloat16)
        stats[d, i, 0:1, :] = top
        stats[d, i, 1:2, :] = total

    def delta_step(d, i, fresh):
        low, high = key_span(d, i)
        prob_grad = dot_t(keys_of(d)[1][low * B : high * B, :], g_heads[i])
        weight = probs[d, i, low * B : high * B, :].astype(jnp.float32)
        stats[d, i, 2:3, :] = jnp.sum(weight * prob_grad, axis=0, keepdims=True)

    def scaled_delta_step(whole_from):
        def step(d, i, fresh):
            delta_step(d, i, fresh)
            done = jnp.logical_or(jnp.int32(d) >= whole_from, jnp.int32(i) == nb - 1)
            stats[d, i, 3:4, :] = jnp.where(done, jnp.float32(1.0), stats[d, i, 1:2, :])

        return step

    def value_step(d, i, fresh):
        low, high = key_span(d, i)
        weight = probs[d, i, low * B : high * B, :].astype(jnp.float32)
        prob_half = (weight * stats[d, i, 1:2, :]).astype(jnp.bfloat16)
        probs[d, i, low * B : high * B, :] = prob_half
        term = dot_n(prob_half, g_heads[i])
        if fresh:
            kv_sum[d, 1, low * B : high * B, :] = term
        else:
            kv_sum[d, 1, low * B : high * B, :] += term

    def grad_step(d, i, fresh):
        low, high = key_span(d, i)
        keys = keys_of(d)[0][low * B : high * B, :]
        prob_grad = dot_t(keys_of(d)[1][low * B : high * B, :], g_heads[i])
        prob = probs[d, i, low * B : high * B, :].astype(jnp.float32)
        score_half = (prob * (prob_grad - delta[i, 0:1, :])).astype(jnp.bfloat16)
        term = dot_n(score_half, q_heads[i])
        if fresh:
            kv_sum[d, 0, low * B : high * B, :] = term
        else:
            kv_sum[d, 0, low * B : high * B, :] += term
        dq_sum[i] += dot_lt(keys, score_half)

    def over_blocks(d, step):
        if d == 0:
            for i in range(nb - 1, -1, -1):
                step(d, i, i == nb - 1)
            return
        step(d, 0, True)
        if d == reach:
            for i in range(1, nb):
                step(d, i, False)
            return

        def one(i, carry):
            step(d, i, False)
            return carry

        lax.fori_loop(1, nb, one, 0)

    def present(d, step, extra=None):
        @pl.when(me >= d if extra is None else (me >= d) & extra)
        def _():
            over_blocks(d, step)

    def arrive(d, c, checked=True):
        there = me >= d if checked else True

        @pl.when(there)
        def _():
            if (d, c) == (reach, 1):
                last_hop(0).wait_recv()
            else:
                forward(d - 1, c).wait_recv()

        if d < reach:

            @pl.when(there & has_next)
            def _():
                if (d, c) == (reach - 1, 1):
                    last_hop(0).start()
                    last_hop(1).start()
                else:
                    forward(d, c).start()

    def take_values(d, step):
        arrive(d, 1, False)
        over_blocks(d, step)

    def scaled(d, c):
        return kv_sum[d, c] * scale if c == 0 else kv_sum[d, c]

    def send_first(d, c, extra=True):
        first = me >= d if d == reach else (me >= d) & jnp.logical_not(has_next) & extra

        @pl.when(first)
        def _():
            ret_out[d - 1, c] = scaled(d, c).astype(jnp.bfloat16)
            backward(d, c).start()

    def send_on(d, c, extra=None):
        @pl.when((me >= d if extra is None else extra) & has_next)
        def _():
            backward(d + 1, c).wait_recv()
            ret_out[d - 1, c] = (scaled(d, c) + ret_in[d, c].astype(jnp.float32)).astype(jnp.bfloat16)
            backward(d, c).start()

    present(0, score_step)
    present(0, delta_step)
    for copy in whole:
        copy.wait()
    for k in range(1, pairs):
        for m in range(2):
            span = span_of(owner_of(k, m == 0))
            turned_ref[k - 1, m, :lead, :] = wq_ref[span, :].T

    @pl.when(jnp.logical_not(has_next))
    def _():
        for k in range(1, pairs):
            for m in range(2):
                span = span_of(owner_of(k, m == 0))
                turned_ref[k - 1, m, lead : lead + HEAD_WIDTH, :] = wk_ref[span, :].T
                turned_ref[k - 1, m, lead + HEAD_WIDTH :, :] = wv_ref[span, :].T

    for d in range(1, reach + 1):
        arrive(d, 0)
        if d == 1:

            @pl.when((me == 1) & (parity == 0) & has_next)
            def _():
                forward(0, 1).start()

        present(d, score_step)
        if d == 1:

            @pl.when((me == 1) & (parity == 1) & has_next)
            def _():
                forward(0, 1).start()

        if d < reach:

            @pl.when(me > d + 1)
            def _():
                take_values(d, delta_step)

    for i in range(nb):
        tops = [stats[d, i, 0:1, :] for d in range(reach + 1)]
        top = functools.reduce(jnp.maximum, tops)
        parts = [jnp.exp2(t - top) for t in tops]
        total = functools.reduce(jnp.add, [parts[d] * stats[d, i, 1:2, :] for d in range(reach + 1)])
        inverse = 1.0 / total
        for d in range(reach + 1):
            stats[d, i, 1:2, :] = parts[d] * inverse
            stats[d, i, 3:4, :] = parts[d] * inverse

    top, second = nb - 1, nb - 2

    def over_near(i, step):
        step(0, i, i == top)

        def one(d, carry):
            step(d, i, i == top)
            return carry

        if reach > 1:
            lax.fori_loop(1, jnp.minimum(me, reach - 1) + 1, one, 0)

    def rest_blocks(d, step, count):
        if d in (0, reach):
            for i in range(count - 1, -1, -1):
                step(d, i, False)
            return

        def one(i, carry):
            step(d, i, False)
            return carry

        lax.fori_loop(0, count, one, 0)

    def over_rest(d, step, count):
        @pl.when(me >= d)
        def _():
            rest_blocks(d, step, count)

    def finish(i):
        part = slice(i * B, (i + 1) * B)
        turned = (dq_sum[i] * scale).T.astype(jnp.bfloat16)
        for h in range(heads):
            dq_ref[part, h * HEAD_WIDTH : (h + 1) * HEAD_WIDTH] = turned[h * B : (h + 1) * B]

        @pl.when(jnp.logical_not(has_next))
        def _():
            for c in range(2):
                own = kv_sum[0, c, part, :] * scale if c == 0 else kv_sum[0, c, part, :]
                dq_ref[part, lead + c * HEAD_WIDTH : lead + (c + 1) * HEAD_WIDTH] = own.astype(jnp.bfloat16)

    half_cols = cols // 2
    piece = math.gcd(cols, 512)
    hold = me + 2 == shards

    def term(owner, part, first, count, keep):
        span = pl.ds(pl.multiple_of(owner * cols + first, count), count)
        value = dot_t(dq_ref[part, :lead], wq_ref[span, :])
        if keep:
            value = value + dot_t(dq_ref[part, lead : lead + HEAD_WIDTH], wk_ref[span, :])
            value = value + dot_t(dq_ref[part, lead + HEAD_WIDTH :], wv_ref[span, :])
        return value

    def far_term(k, m, part, keep):
        depth = lead + 2 * HEAD_WIDTH if keep else lead
        return dot_n(dq_ref[part, :depth], turned_ref[k - 1, m, :depth, :])

    def to_pair(k, c, h):
        return pltpu.make_async_remote_copy(
            src_ref=pair_out.at[k - 1, c, h],
            dst_ref=pair_in.at[k - 1, c, h],
            send_sem=pair_send.at[k - 1, c, h],
            recv_sem=pair_recv.at[k - 1, c, h],
            device_id={"tp": partner},
            device_id_type=MESH_ID,
        )

    def to_far(k, c, h):
        return pltpu.make_async_remote_copy(
            src_ref=far_out.at[k - 1, c, h],
            dst_ref=far_in.at[k - 1, c, h],
            send_sem=far_send.at[k - 1, c, h],
            recv_sem=far_recv.at[k - 1, c, h],
            device_id={"tp": peer_of(k)},
            device_id_type=MESH_ID,
        )

    def to_near(n):
        return pltpu.make_async_remote_copy(
            src_ref=near_out.at[n],
            dst_ref=near_in.at[n],
            send_sem=near_send.at[n],
            recv_sem=near_recv.at[n],
            device_id={"tp": partner},
            device_id_type=MESH_ID,
        )

    def both(step):
        @pl.when(has_next)
        def _():
            step(False)

        @pl.when(jnp.logical_not(has_next))
        def _():
            step(True)

    def far_give(low, count):
        part = slice(low * B, (low + count) * B)

        def step(keep):
            for k in range(1, pairs):
                value = far_term(k, 1, part, keep).astype(jnp.bfloat16)
                for n in range(count - 1, -1, -1):
                    for h in range(2):
                        pair_out[k - 1, low + n, h] = value[n * B : (n + 1) * B, h * half_cols : (h + 1) * half_cols]
                        to_pair(k, low + n, h).start()

        both(step)

    def far_take(low, count, which):
        part = slice(low * B, (low + count) * B)

        def step(keep):
            for k in range(1, pairs):
                value = far_term(k, 0, part, keep)
                for n in range(count - 1, -1, -1):
                    for h in range(2):
                        c = low + n
                        to_pair(k, c, h).wait_recv()
                        total = value[n * B : (n + 1) * B, h * half_cols : (h + 1) * half_cols]
                        total = total + pair_in[k - 1, c, h].astype(jnp.float32)
                        far_out[k - 1, c, h] = total.astype(jnp.bfloat16)
                        if keep or (c, h) != (0, 1):
                            to_far(k, c, h).start()
                        else:

                            @pl.when(jnp.logical_not(hold))
                            def _():
                                to_far(k, c, h).start()

        @pl.when(parity == which)
        def _():
            both(step)

    def near_give():
        def step(keep):
            for n in range(cols // piece):
                near_out[n] = term(partner, slice(0, rows), n * piece, piece, keep).astype(jnp.bfloat16)
                to_near(n).start()

        both(step)

    def near_take():
        def step(keep):
            for n in range(cols // piece):
                value = term(place, slice(0, rows), n * piece, piece, keep)
                to_near(n).wait_recv()
                near_sum[:, n * piece : (n + 1) * piece] = value + near_in[n].astype(jnp.float32)

        both(step)

    def gather(k, m, c):
        return pltpu.make_async_remote_copy(
            src_ref=dkv_all.at[c, :, slot(k, 0)] if m == 1 else dkv_all.at[c, :, slot(0, 0)],
            dst_ref=dkv_all.at[c, :, slot(k, m)],
            send_sem=gather_send.at[k, m, c],
            recv_sem=gather_recv.at[k, m, c],
            device_id={"tp": partner if m == 1 else peer_of(k)},
            device_id_type=MESH_ID,
        )

    def settle(c, extra=True):
        @pl.when(has_next & extra)
        def _():
            backward(1, c).wait_recv()
            dkv_all[c, :, 0:HEAD_WIDTH] = (scaled(0, c) + ret_in[0, c].astype(jnp.float32)).astype(jnp.bfloat16)
            for k in range(1, pairs):
                gather(k, 0, c).start()
            gather(0, 1, c).start()

    def add_terms(k, c):
        lanes = slice(2 * k * HEAD_WIDTH, (2 * k + 2) * HEAD_WIDTH)
        step_cols = min(256, cols)
        for n in range(0, cols, step_cols):
            near_sum[:, n : n + step_cols] += dot_t(dkv_all[c, :, lanes], kw_all[c, n : n + step_cols, lanes])

    def near_adds(c):
        gather(0, 1, c).wait_recv()
        add_terms(0, c)

    def far_passes(c):
        for k in range(1, pairs):
            gather(k, 0, c).wait_recv()
            gather(k, 1, c).start()

    def far_adds(c):
        for k in range(1, pairs):
            gather(k, 1, c).wait_recv()
            add_terms(k, c)

    present(reach, value_step)
    send_first(reach, 1)
    over_near(top, value_step)


    for d in range(reach - 1, 0, -1):

        @pl.when(me >= reach)
        def _():
            rest_blocks(d, value_step, top)

        send_first(d, 1)

    def late_deltas(step):
        for d in range(1, reach):

            @pl.when(me == d + 1)
            def _():
                step(d, scaled_delta_step(reach - 1 if d == reach - 1 else reach))

        for d in range(1, reach + 1):

            @pl.when(me >= reach if d == reach else me == d)
            def _():
                step(d, scaled_delta_step(reach))

    def late_top(d, step):
        arrive(d, 1, False)
        step(d, top, False)

    late_deltas(late_top)

    def sum_delta(i):
        delta[i, 0:1, :] = functools.reduce(
            jnp.add, [stats[d, i, 3:4, :] * stats[d, i, 2:3, :] for d in range(reach + 1)]
        )

    sum_delta(top)
    over_near(top, grad_step)

    @pl.when(me >= reach)
    def _():
        grad_step(reach, top, False)

    finish(top)
    far_give(top, 1)
    far_take(top, 1, 0)

    if relayed:

        @pl.when(has_next)
        def _():
            for c in (1, 0):
                for k in range(1, pairs):
                    fetch(k, group, c).wait_recv()
                    relay(k, c).start()

    def late_rest(d, step):
        if d == reach:

            @pl.when(me >= reach)
            def _():
                last_hop(1).wait_recv()

        rest_blocks(d, step, top)

    def second_value(d, i, fresh):
        if isinstance(d, int):
            value_step(d, i, fresh)
        else:

            @pl.when(me < reach)
            def _():
                value_step(d, i, fresh)

    late_deltas(late_rest)
    for i in range(top):
        sum_delta(i)
    over_rest(reach, grad_step, top)
    send_first(reach, 0)
    far_take(top, 1, 1)
    over_near(second, second_value)
    over_near(second, grad_step)
    finish(second)
    far_give(second, 1)
    far_take(second, 1, 0)
    for d in range(reach - 1, 0, -1):

        @pl.when((me >= d) & (me < reach))
        def _():
            rest_blocks(d, value_step, second)

        if reach > 1:
            send_on(d, 1, me >= max(d, 2))
        over_rest(d, grad_step, second)
        send_first(d, 0)
        if d == reach - 1:
            far_take(second, 1, 1)
    over_rest(0, value_step, second)
    over_rest(0, grad_step, second)
    for i in range(second):
        finish(i)
    far_give(0, second)
    far_take(0, second, 0)
    far_take(0, second, 1)
    near_give()
    for d in range(reach - 1, 1, -1):
        send_on(d, 0)
    near_take()
    if reach > 1:
        send_on(1, 1, me == 1)
    settle(1, me >= 2)
    if reach > 1:
        send_on(1, 0)
    settle(1, me < 2)

    @pl.when(has_next)
    def _():
        for c in range(2):
            own_weights(c).wait()
            fetch(0, 1, c).wait_recv()
        near_adds(1)

    settle(0)

    @pl.when(has_next)
    def _():
        @pl.when(hold)
        def _():
            for k in range(1, pairs):
                to_far(k, 0, 1).start()

        for k in range(1, pairs):
            for c in range(2):
                if relayed:
                    relay(k, c, True).wait_recv()
                else:
                    for m in range(2):
                        fetch(k, m, c).wait_recv()
        far_passes(1)
        near_adds(0)
        far_adds(1)
        far_passes(0)
        far_adds(0)

    near = list(range(nb - 1, -1, -1))
    for c in near:
        for h in range(2):
            part = (slice(c * B, (c + 1) * B), slice(h * half_cols, (h + 1) * half_cols))
            value = near_sum[part]
            for k in range(1, pairs):
                to_far(k, c, h).wait_recv()
                value = value + far_in[k - 1, c, h].astype(jnp.float32)
            out_ref[part] = value.astype(jnp.bfloat16)

    @pl.when(has_next)
    def _():
        for k, m in others:
            for c in range(2):
                gather(k, m, c).wait_send()
        for item in fetches:
            fetch(*item).wait_send()
        if relayed:
            for k in range(1, pairs):
                for c in range(2):
                    relay(k, c).wait_send()

    for c in near:
        for h in range(2):
            for k in range(1, pairs):
                to_pair(k, c, h).wait_send()
                to_far(k, c, h).wait_send()
    for n in range(cols // piece):
        to_near(n).wait_send()

    for d in range(reach):

        @pl.when((me >= d) & has_next)
        def _():
            forward(d, 0).wait_send()
            if d == reach - 1:
                last_hop(0).wait_send()
                last_hop(1).wait_send()
            else:
                forward(d, 1).wait_send()

        @pl.when(me >= d + 1)
        def _():
            for c in range(2):
                backward(d + 1, c).wait_send()


def body(
    query,
    key_head_rows,
    value_head_rows,
    output_gradient,
    doc_blocks,
    w_query,
    key_weight,
    value_weight,
):
    shards = lax.axis_size("seq")
    places = lax.axis_size("tp")
    groups = lax.axis_size("groups")
    pairs = places // 2
    reach = min(8, shards - 1)
    rows, q_width = query.shape
    nb = rows // BLOCK_POSITIONS
    cols = w_query.shape[0] // places
    width = (q_width // HEAD_WIDTH) * BLOCK_POSITIONS
    half, full = jnp.bfloat16, jnp.float32
    vmem = pl.BlockSpec(memory_space=pltpu.VMEM)
    hbm = pl.BlockSpec(memory_space=pltpu.HBM)
    dma = pltpu.SemaphoreType.DMA
    buffers = [
        ((rows, q_width), half),
        ((rows, HEAD_WIDTH), half),
        ((rows, HEAD_WIDTH), half),
        ((rows, q_width), half),
        ((rows, q_width + 2 * HEAD_WIDTH), half),
        ((pairs - 1, 2, q_width + 2 * HEAD_WIDTH, cols), half),
        ((2, rows, 2 * pairs * HEAD_WIDTH), half),
        ((2, cols, 2 * pairs * HEAD_WIDTH), half),
        (w_query.shape, half),
        (key_weight.shape, half),
        (value_weight.shape, half),
        ((rows, cols), full),
        ((cols // math.gcd(cols, 512), rows, math.gcd(cols, 512)), half),
        ((cols // math.gcd(cols, 512), rows, math.gcd(cols, 512)), half),
        ((pairs - 1, nb, 2, rows // nb, cols // 2), half),
        ((pairs - 1, nb, 2, rows // nb, cols // 2), half),
        ((pairs - 1, nb, 2, rows // nb, cols // 2), half),
        ((pairs - 1, nb, 2, rows // nb, cols // 2), half),
    ]
    later = [
        ((reach, 2, rows, HEAD_WIDTH), half),
        ((nb, width, HEAD_WIDTH), half),
        ((nb, width, HEAD_WIDTH), half),
        ((reach + 1, nb, 8, width), full),
        ((nb, 8, width), full),
        ((nb, HEAD_WIDTH, width), full),
        ((reach + 1, nb, rows, width), half),
        ((reach + 1, 2, rows, HEAD_WIDTH), full),
        ((reach, 2, rows, HEAD_WIDTH), half),
        ((reach, 2, rows, HEAD_WIDTH), half),
    ]
    used = sum(math.prod(shape) * jnp.dtype(kind).itemsize for shape, kind in buffers + later)
    limit = min(used + SPARE_MIB * 1024 * 1024, 60 * 1024 * 1024)
    return pl.pallas_call(
        functools.partial(attention_kernel, shards, reach, places, groups),
        out_shape=jax.ShapeDtypeStruct((rows, cols), half),
        in_specs=[hbm] * 8,
        out_specs=vmem,
        scratch_shapes=[pltpu.SMEM(doc_blocks.shape, doc_blocks.dtype)]
        + [pltpu.VMEM(*item) for item in buffers]
        + [
            dma((5,)),
            dma((3,)),
            dma((cols // math.gcd(cols, 512),)),
            dma((cols // math.gcd(cols, 512),)),
            dma((pairs - 1, nb, 2)),
            dma((pairs - 1, nb, 2)),
            dma((pairs - 1, nb, 2)),
            dma((pairs - 1, nb, 2)),
            dma((pairs, 2, 2)),
            dma((pairs, 2, 2)),
            dma((pairs, 2)),
            dma((pairs, 2)),
            dma((pairs, 2, 2)),
            dma((pairs, 2, 2)),
        ]
        + [pltpu.VMEM(*item) for item in later]
        + [
            dma((reach, 2)),
            dma((reach, 2)),
            dma((2,)),
            dma((2,)),
            dma((reach, 2)),
            dma((reach, 2)),
        ],
        compiler_params=pltpu.CompilerParams(
            collective_id=0, has_side_effects=True, vmem_limit_bytes=limit
        ),
        name="attention",
    )(
        pltpu.with_memory_space_constraint(query, pltpu.HBM),
        pltpu.with_memory_space_constraint(key_head_rows, pltpu.HBM),
        pltpu.with_memory_space_constraint(value_head_rows, pltpu.HBM),
        pltpu.with_memory_space_constraint(output_gradient, pltpu.HBM),
        pltpu.with_memory_space_constraint(doc_blocks, pltpu.HBM),
        pltpu.with_memory_space_constraint(w_query, pltpu.HBM),
        pltpu.with_memory_space_constraint(key_weight, pltpu.HBM),
        pltpu.with_memory_space_constraint(value_weight, pltpu.HBM),
    )


def solution(mesh):
    in_specs = (
        P(("groups", "seq"), "tp"),
        P(("groups", "seq"), "tp"),
        P(("groups", "seq"), "tp"),
        P(("groups", "seq"), "tp"),
        P(("groups", "seq"), None),
        P(None, "tp"),
        P(None, "tp"),
        P(None, "tp"),
    )
    out_specs = P(("groups", "seq"), "tp")
    return jax.shard_map(body, mesh=mesh, in_specs=in_specs, out_specs=out_specs, check_vma=False)
```

```python
import functools
import math

import jax
import jax.numpy as jnp
from jax import lax
from jax.experimental import pallas as pl
from jax.experimental.pallas import tpu as pltpu
from jax.sharding import PartitionSpec as P

HEAD_WIDTH = 128
BLOCK_POSITIONS = 128
MESH_ID = pl.DeviceIdType.MESH
SPARE_MIB = 12


def dot_t(a, b):
    return lax.dot_general(a, b, (((1,), (1,)), ((), ())), preferred_element_type=jnp.float32)


def dot_n(a, b):
    return lax.dot_general(a, b, (((1,), (0,)), ((), ())), preferred_element_type=jnp.float32)


def dot_lt(a, b):
    return lax.dot_general(a, b, (((0,), (0,)), ((), ())), preferred_element_type=jnp.float32)


FLOOR = -1e9


def attention_kernel(
    shards,
    reach,
    places,
    groups,
    q_hbm,
    k_hbm,
    v_hbm,
    g_hbm,
    docs_hbm,
    wq_hbm,
    wk_hbm,
    wv_hbm,
    out_ref,
    docs_ref,
    q_ref,
    k_ref,
    v_ref,
    g_ref,
    dq_ref,
    turned_ref,
    dkv_all,
    kw_all,
    wq_ref,
    wk_ref,
    wv_ref,
    near_sum,
    near_out,
    near_in,
    pair_out,
    pair_in,
    far_out,
    far_in,
    load_sem,
    weight_sem,
    near_send,
    near_recv,
    pair_send,
    pair_recv,
    far_send,
    far_recv,
    fetch_send,
    fetch_recv,
    relay_send,
    relay_recv,
    gather_send,
    gather_recv,
    kv_win,
    q_heads,
    g_heads,
    stats,
    delta,
    dq_sum,
    probs,
    kv_sum,
    ret_out,
    ret_in,
    send_sem,
    recv_sem,
    last_send,
    last_recv,
    ret_send,
    ret_recv,
):
    B = BLOCK_POSITIONS
    rows = k_ref.shape[0]
    nb = rows // B
    heads = q_ref.shape[1] // HEAD_WIDTH
    lead = q_ref.shape[1]
    listed_count = docs_ref.shape[1]
    me = lax.axis_index("seq")
    scale = HEAD_WIDTH ** -0.5
    scale2 = scale * math.log2(math.e)
    has_next = me + 1 < shards
    has_prev = me >= 1

    pairs = places // 2
    place = lax.axis_index("tp")
    my_pair = place // 2
    parity = place % 2
    partner = my_pair * 2 + 1 - parity
    cols = out_ref.shape[1]
    relayed = groups == 2
    group = lax.axis_index("groups")

    def peer_of(k):
        return lax.rem(my_pair + k, pairs) * 2 + parity

    def owner_of(k, mine):
        return lax.rem(my_pair + k, pairs) * 2 + (parity if mine else 1 - parity)

    loads = [
        pltpu.make_async_copy(src, dst, load_sem.at[n])
        for n, (src, dst) in enumerate(((k_hbm, k_ref), (q_hbm, q_ref), (v_hbm, v_ref), (g_hbm, g_ref), (docs_hbm, docs_ref)))
    ]
    whole = [
        pltpu.make_async_copy(wq_hbm, wq_ref, weight_sem.at[0]),
        pltpu.make_async_copy(wk_hbm, wk_ref, weight_sem.at[1]),
        pltpu.make_async_copy(wv_hbm, wv_ref, weight_sem.at[2]),
    ]
    for copy in loads + whole:
        copy.start()

    barrier = pltpu.get_barrier_semaphore()
    others = [(k, m) for k in range(pairs) for m in range(2) if (k, m) != (0, 0)]
    for k, m in others:
        pl.semaphore_signal(barrier, inc=1, device_id={"tp": owner_of(k, m == 0)}, device_id_type=MESH_ID)
    if relayed:
        pl.semaphore_signal(barrier, inc=1, device_id={"groups": 1 - group}, device_id_type=MESH_ID)

    @pl.when(has_next)
    def _():
        pl.semaphore_signal(barrier, inc=1, device_id={"seq": me + 1}, device_id_type=MESH_ID)

    @pl.when(has_prev)
    def _():
        pl.semaphore_signal(barrier, inc=1, device_id={"seq": me - 1}, device_id_type=MESH_ID)

    greeted = places - 1 + (1 if relayed else 0)
    pl.semaphore_wait(barrier, has_next.astype(jnp.int32) + has_prev.astype(jnp.int32) + greeted)

    def forward(d, c):
        src = (k_hbm, v_hbm)[c] if d == 0 else kv_win.at[d - 1, c]
        return pltpu.make_async_remote_copy(
            src_ref=src,
            dst_ref=kv_win.at[d, c],
            send_sem=send_sem.at[d, c],
            recv_sem=recv_sem.at[d, c],
            device_id={"seq": jnp.minimum(me + 1, shards - 1)},
            device_id_type=MESH_ID,
        )

    def last_hop(n):
        span = pl.ds(rows - B, B) if n == 0 else pl.ds(0, rows - B)
        return pltpu.make_async_remote_copy(
            src_ref=(v_hbm if reach == 1 else kv_win.at[reach - 2, 1]).at[span],
            dst_ref=kv_win.at[reach - 1, 1, span],
            send_sem=last_send.at[n],
            recv_sem=last_recv.at[n],
            device_id={"seq": jnp.minimum(me + 1, shards - 1)},
            device_id_type=MESH_ID,
        )

    spans = [slice(n * (rows // 2), (n + 1) * (rows // 2)) for n in range(2)]

    def backward(d, c, n):
        return pltpu.make_async_remote_copy(
            src_ref=ret_out.at[d - 1, c, spans[n]],
            dst_ref=ret_in.at[d - 1, c, spans[n]],
            send_sem=ret_send.at[d - 1, c, n],
            recv_sem=ret_recv.at[d - 1, c, n],
            device_id={"seq": jnp.maximum(me - 1, 0)},
            device_id_type=MESH_ID,
        )

    def span_of(owner):
        return pl.ds(pl.multiple_of(owner * cols, cols), cols)

    def slot(k, m):
        lane = (2 * k + m) * HEAD_WIDTH
        return pl.ds(lane if isinstance(m, int) else pl.multiple_of(lane, HEAD_WIDTH), HEAD_WIDTH)

    def fetch(k, m, c):
        if isinstance(m, int):
            owner = owner_of(k, m == 0)
        else:
            owner = lax.rem(my_pair + k, pairs) * 2 + lax.rem(parity + m, 2)
        return pltpu.make_async_remote_copy(
            src_ref=(wk_hbm, wv_hbm)[c].at[span_of(owner)],
            dst_ref=kw_all.at[c, :, slot(k, m)],
            send_sem=fetch_send.at[k, m, c],
            recv_sem=fetch_recv.at[k, m, c],
            device_id={"tp": owner},
            device_id_type=MESH_ID,
        )

    def own_weights(c):
        return pltpu.make_async_copy(
            (wk_hbm, wv_hbm)[c].at[span_of(place)], kw_all.at[c, :, slot(0, 0)], fetch_recv.at[0, 0, c]
        )

    def relay(k, c, arriving=False):
        which = 1 - group if arriving else group
        return pltpu.make_async_remote_copy(
            src_ref=kw_all.at[c, :, slot(k, which)],
            dst_ref=kw_all.at[c, :, slot(k, which)],
            send_sem=relay_send.at[k, c],
            recv_sem=relay_recv.at[k, c],
            device_id={"groups": 1 - group},
            device_id_type=MESH_ID,
        )

    if relayed:
        fetches = [(0, 1, c) for c in range(2)] + [(k, group, c) for c in (1, 0) for k in range(1, pairs)]
    else:
        fetches = [(k, m, c) for k, m in others for c in range(2)]

    @pl.when(has_next)
    def _():
        forward(0, 0).start()

        @pl.when((me != 1) | (parity == 0))
        def _():
            forward(0, 1).start()

        for item in fetches:
            fetch(*item).start()
        for c in range(2):
            own_weights(c).start()

    width = heads * B
    for d in range(1, reach + 1):
        for i in range(nb):
            stats[d, i, 0:1, :] = jnp.full((1, width), FLOOR, jnp.float32)
            stats[d, i, 1:3, :] = jnp.zeros((2, width), jnp.float32)

    for i in range(nb):
        dq_sum[i] = jnp.zeros((HEAD_WIDTH, width), jnp.float32)

    @pl.when(me >= reach)
    def _():
        kv_sum[reach, 0] = jnp.zeros((rows, HEAD_WIDTH), jnp.float32)

    for copy in loads:
        copy.wait()
    for i in range(nb):
        for h in range(heads):
            q_heads[i, h * B : (h + 1) * B, :] = q_ref[i * B : (i + 1) * B, h * HEAD_WIDTH : (h + 1) * HEAD_WIDTH]
            g_heads[i, h * B : (h + 1) * B, :] = g_ref[i * B : (i + 1) * B, h * HEAD_WIDTH : (h + 1) * HEAD_WIDTH]
    key_row = lax.broadcasted_iota(jnp.int32, (B, width), 0)
    query_row = lax.broadcasted_iota(jnp.int32, (B, width), 1) & (B - 1)
    own_mask = key_row <= query_row

    def keys_of(d):
        if isinstance(d, int) and d == 0:
            return k_ref, v_ref
        return kv_win.at[d - 1, 0], kv_win.at[d - 1, 1]

    def key_span(d, i):
        if isinstance(i, int) and isinstance(d, int) and d == 0:
            return 0, i + 1
        if isinstance(i, int) and isinstance(d, int) and d == reach:
            return i, nb
        return 0, nb

    def biased(d, i, j, raw):
        offset = d * nb + i - j
        if isinstance(i, int) and offset == 0:
            return jnp.where(own_mask, raw, -jnp.inf), jnp.float32(0.0)
        if isinstance(i, int) and offset == 1:
            return jnp.where(own_mask, -jnp.inf, raw), jnp.float32(0.0)
        key_block = (me - d) * nb + j
        hits = jnp.int32(0)
        for n in range(listed_count):
            hits = hits | (docs_ref[i, n] == key_block).astype(jnp.int32)
        ok = (hits > 0) & (offset >= 2)
        return raw, jnp.where(ok, jnp.float32(0.0), jnp.float32(-jnp.inf))

    def raw_blocks(d, i):
        low, high = key_span(d, i)
        raw = dot_t(keys_of(d)[0][low * B : high * B, :], q_heads[i])
        return [
            biased(d, i, j, raw[(j - low) * B : (j - low + 1) * B]) for j in range(low, high)
        ]

    def score_step(d, i, fresh):
        low, high = key_span(d, i)
        blocks = raw_blocks(d, i)
        tops = [jnp.max(raw, axis=0, keepdims=True) * scale2 + bias for raw, bias in blocks]
        top = jnp.maximum(functools.reduce(jnp.maximum, tops), FLOOR)
        total = 0.0
        for j, (raw, bias) in enumerate(blocks):
            weight = jnp.exp2(raw * scale2 + (bias - top))
            total = total + jnp.sum(weight, axis=0, keepdims=True)
            probs[d, i, (low + j) * B : (low + j + 1) * B, :] = weight.astype(jnp.bfloat16)
        stats[d, i, 0:1, :] = top
        stats[d, i, 1:2, :] = total

    def delta_step(d, i, fresh):
        low, high = key_span(d, i)
        prob_grad = dot_t(keys_of(d)[1][low * B : high * B, :], g_heads[i])
        weight = probs[d, i, low * B : high * B, :].astype(jnp.float32)
        stats[d, i, 2:3, :] = jnp.sum(weight * prob_grad, axis=0, keepdims=True)

    def scaled_delta_step(whole_from):
        def step(d, i, fresh):
            delta_step(d, i, fresh)
            done = jnp.logical_or(jnp.int32(d) >= whole_from, jnp.int32(i) == nb - 1)
            stats[d, i, 3:4, :] = jnp.where(done, jnp.float32(1.0), stats[d, i, 1:2, :])

        return step

    def value_step(d, i, fresh):
        low, high = key_span(d, i)
        weight = probs[d, i, low * B : high * B, :].astype(jnp.float32)
        prob_half = (weight * stats[d, i, 1:2, :]).astype(jnp.bfloat16)
        probs[d, i, low * B : high * B, :] = prob_half
        term = dot_n(prob_half, g_heads[i])
        if fresh:
            kv_sum[d, 1, low * B : high * B, :] = term
        else:
            kv_sum[d, 1, low * B : high * B, :] += term

    def grad_step(d, i, fresh):
        low, high = key_span(d, i)
        keys = keys_of(d)[0][low * B : high * B, :]
        prob_grad = dot_t(keys_of(d)[1][low * B : high * B, :], g_heads[i])
        prob = probs[d, i, low * B : high * B, :].astype(jnp.float32)
        score_half = (prob * (prob_grad - delta[i, 0:1, :])).astype(jnp.bfloat16)
        term = dot_n(score_half, q_heads[i])
        if fresh:
            kv_sum[d, 0, low * B : high * B, :] = term
        else:
            kv_sum[d, 0, low * B : high * B, :] += term
        dq_sum[i] += dot_lt(keys, score_half)

    def over_blocks(d, step):
        if d == 0:
            for i in range(nb - 1, -1, -1):
                step(d, i, i == nb - 1)
            return
        step(d, 0, True)
        if d == reach:
            for i in range(1, nb):
                step(d, i, False)
            return

        def one(i, carry):
            step(d, i, False)
            return carry

        lax.fori_loop(1, nb, one, 0)

    def present(d, step, extra=None):
        @pl.when(me >= d if extra is None else (me >= d) & extra)
        def _():
            over_blocks(d, step)

    def arrive(d, c, checked=True):
        there = me >= d if checked else True

        @pl.when(there)
        def _():
            if (d, c) == (reach, 1):
                last_hop(0).wait_recv()
            else:
                forward(d - 1, c).wait_recv()

        if d < reach:

            @pl.when(there & has_next)
            def _():
                if (d, c) == (reach - 1, 1):
                    last_hop(0).start()
                    last_hop(1).start()
                else:
                    forward(d, c).start()

    def take_values(d, step):
        arrive(d, 1, False)
        over_blocks(d, step)

    def scaled(d, c, n):
        return kv_sum[d, c, spans[n]] * scale if c == 0 else kv_sum[d, c, spans[n]]

    def send_first(d, c, extra=True):
        first = me >= d if d == reach else (me >= d) & jnp.logical_not(has_next) & extra

        @pl.when(first)
        def _():
            for n in range(2):
                ret_out[d - 1, c, spans[n]] = scaled(d, c, n).astype(jnp.bfloat16)
                backward(d, c, n).start()

    def send_on(d, c, extra=None):
        @pl.when((me >= d if extra is None else extra) & has_next)
        def _():
            for n in range(2):
                backward(d + 1, c, n).wait_recv()
                total = scaled(d, c, n) + ret_in[d, c, spans[n]].astype(jnp.float32)
                ret_out[d - 1, c, spans[n]] = total.astype(jnp.bfloat16)
                backward(d, c, n).start()

    present(0, score_step)
    present(0, delta_step)
    for copy in whole:
        copy.wait()
    for k in range(1, pairs):
        for m in range(2):
            span = span_of(owner_of(k, m == 0))
            turned_ref[k - 1, m, :lead, :] = wq_ref[span, :].T

    @pl.when(jnp.logical_not(has_next))
    def _():
        for k in range(1, pairs):
            for m in range(2):
                span = span_of(owner_of(k, m == 0))
                turned_ref[k - 1, m, lead : lead + HEAD_WIDTH, :] = wk_ref[span, :].T
                turned_ref[k - 1, m, lead + HEAD_WIDTH :, :] = wv_ref[span, :].T

    for d in range(1, reach + 1):
        arrive(d, 0)
        present(d, score_step)
        if d == 1:

            @pl.when((me == 1) & (parity == 1) & has_next)
            def _():
                forward(0, 1).start()

        if d < reach:

            @pl.when(me > d + 1)
            def _():
                take_values(d, delta_step)

    for i in range(nb):
        tops = [stats[d, i, 0:1, :] for d in range(reach + 1)]
        top = functools.reduce(jnp.maximum, tops)
        parts = [jnp.exp2(t - top) for t in tops]
        total = functools.reduce(jnp.add, [parts[d] * stats[d, i, 1:2, :] for d in range(reach + 1)])
        inverse = 1.0 / total
        for d in range(reach + 1):
            stats[d, i, 1:2, :] = parts[d] * inverse
            stats[d, i, 3:4, :] = parts[d] * inverse

    top, second = nb - 1, nb - 2

    def over_near(i, step):
        step(0, i, i == top)

        def one(d, carry):
            step(d, i, i == top)
            return carry

        if reach > 1:
            lax.fori_loop(1, jnp.minimum(me, reach - 1) + 1, one, 0)

    def rest_blocks(d, step, count):
        if d in (0, reach):
            for i in range(count - 1, -1, -1):
                step(d, i, False)
            return

        if reach <= 3 and count <= 2:
            for i in range(count):
                step(d, i, False)
            return

        def one(i, carry):
            step(d, i, False)
            return carry

        lax.fori_loop(0, count, one, 0)

    def over_rest(d, step, count):
        @pl.when(me >= d)
        def _():
            rest_blocks(d, step, count)

    def finish(i):
        part = slice(i * B, (i + 1) * B)
        turned = (dq_sum[i] * scale).T.astype(jnp.bfloat16)
        for h in range(heads):
            dq_ref[part, h * HEAD_WIDTH : (h + 1) * HEAD_WIDTH] = turned[h * B : (h + 1) * B]

        @pl.when(jnp.logical_not(has_next))
        def _():
            for c in range(2):
                own = kv_sum[0, c, part, :] * scale if c == 0 else kv_sum[0, c, part, :]
                dq_ref[part, lead + c * HEAD_WIDTH : lead + (c + 1) * HEAD_WIDTH] = own.astype(jnp.bfloat16)

    half_cols = cols // 2
    piece = math.gcd(cols, 512)
    hold = me + 2 == shards

    def term(owner, part, first, count, keep):
        span = pl.ds(pl.multiple_of(owner * cols + first, count), count)
        value = dot_t(dq_ref[part, :lead], wq_ref[span, :])
        if keep:
            value = value + dot_t(dq_ref[part, lead : lead + HEAD_WIDTH], wk_ref[span, :])
            value = value + dot_t(dq_ref[part, lead + HEAD_WIDTH :], wv_ref[span, :])
        return value

    def far_term(k, m, part, keep):
        depth = lead + 2 * HEAD_WIDTH if keep else lead
        return dot_n(dq_ref[part, :depth], turned_ref[k - 1, m, :depth, :])

    def to_pair(k, c, h):
        return pltpu.make_async_remote_copy(
            src_ref=pair_out.at[k - 1, c, h],
            dst_ref=pair_in.at[k - 1, c, h],
            send_sem=pair_send.at[k - 1, c, h],
            recv_sem=pair_recv.at[k - 1, c, h],
            device_id={"tp": partner},
            device_id_type=MESH_ID,
        )

    def to_far(k, c, h):
        return pltpu.make_async_remote_copy(
            src_ref=far_out.at[k - 1, c, h],
            dst_ref=far_in.at[k - 1, c, h],
            send_sem=far_send.at[k - 1, c, h],
            recv_sem=far_recv.at[k - 1, c, h],
            device_id={"tp": peer_of(k)},
            device_id_type=MESH_ID,
        )

    def to_near(n):
        return pltpu.make_async_remote_copy(
            src_ref=near_out.at[n],
            dst_ref=near_in.at[n],
            send_sem=near_send.at[n],
            recv_sem=near_recv.at[n],
            device_id={"tp": partner},
            device_id_type=MESH_ID,
        )

    def both(step):
        @pl.when(has_next)
        def _():
            step(False)

        @pl.when(jnp.logical_not(has_next))
        def _():
            step(True)

    def far_give(low, count):
        part = slice(low * B, (low + count) * B)

        def step(keep):
            for k in range(1, pairs):
                value = far_term(k, 1, part, keep).astype(jnp.bfloat16)
                for n in range(count - 1, -1, -1):
                    for h in range(2):
                        pair_out[k - 1, low + n, h] = value[n * B : (n + 1) * B, h * half_cols : (h + 1) * half_cols]
                        to_pair(k, low + n, h).start()

        both(step)

    def far_take(low, count, which):
        part = slice(low * B, (low + count) * B)

        def step(keep):
            for k in range(1, pairs):
                value = far_term(k, 0, part, keep)
                for n in range(count - 1, -1, -1):
                    for h in range(2):
                        c = low + n
                        to_pair(k, c, h).wait_recv()
                        total = value[n * B : (n + 1) * B, h * half_cols : (h + 1) * half_cols]
                        total = total + pair_in[k - 1, c, h].astype(jnp.float32)
                        far_out[k - 1, c, h] = total.astype(jnp.bfloat16)
                        if keep or (c, h) != (0, 1):
                            to_far(k, c, h).start()
                        else:

                            @pl.when(jnp.logical_not(hold))
                            def _():
                                to_far(k, c, h).start()

        @pl.when(parity == which)
        def _():
            both(step)

    def near_give():
        def step(keep):
            for n in range(cols // piece):
                near_out[n] = term(partner, slice(0, rows), n * piece, piece, keep).astype(jnp.bfloat16)
                to_near(n).start()

        both(step)

    def near_take():
        def step(keep):
            for n in range(cols // piece):
                value = term(place, slice(0, rows), n * piece, piece, keep)
                to_near(n).wait_recv()
                near_sum[:, n * piece : (n + 1) * piece] = value + near_in[n].astype(jnp.float32)

        both(step)

    def gather(k, m, c, n):
        return pltpu.make_async_remote_copy(
            src_ref=dkv_all.at[c, spans[n], slot(k, 0)] if m == 1 else dkv_all.at[c, spans[n], slot(0, 0)],
            dst_ref=dkv_all.at[c, spans[n], slot(k, m)],
            send_sem=gather_send.at[k, m, c, n],
            recv_sem=gather_recv.at[k, m, c, n],
            device_id={"tp": partner if m == 1 else peer_of(k)},
            device_id_type=MESH_ID,
        )

    def settle(c, extra=True):
        @pl.when(has_next & extra)
        def _():
            for n in range(2):
                backward(1, c, n).wait_recv()
                total = scaled(0, c, n) + ret_in[0, c, spans[n]].astype(jnp.float32)
                dkv_all[c, spans[n], 0:HEAD_WIDTH] = total.astype(jnp.bfloat16)
                for k in range(1, pairs):
                    gather(k, 0, c, n).start()
            for n in range(2):
                gather(0, 1, c, n).start()

    def add_terms(k, c):
        lanes = slice(2 * k * HEAD_WIDTH, (2 * k + 2) * HEAD_WIDTH)
        step_cols = min(256, cols)
        for n in range(0, cols, step_cols):
            near_sum[:, n : n + step_cols] += dot_t(dkv_all[c, :, lanes], kw_all[c, n : n + step_cols, lanes])

    def near_adds(c):
        for n in range(2):
            gather(0, 1, c, n).wait_recv()
        add_terms(0, c)

    def far_passes(c):
        for k in range(1, pairs):
            for n in range(2):
                gather(k, 0, c, n).wait_recv()
                gather(k, 1, c, n).start()

    def far_adds(c):
        for k in range(1, pairs):
            for n in range(2):
                gather(k, 1, c, n).wait_recv()
            add_terms(k, c)

    present(reach, value_step)
    send_first(reach, 1)
    over_near(top, value_step)


    if reach > 1:

        @pl.when(me >= reach)
        def _():
            rest_blocks(reach - 1, value_step, top)

        send_first(reach - 1, 1, me >= reach)

    def late_deltas(step):
        for d in range(1, reach):

            @pl.when(me == d + 1)
            def _():
                step(d, scaled_delta_step(reach - 1 if d == reach - 1 else reach))

        for d in range(1, reach + 1):

            @pl.when(me >= reach if d == reach else me == d)
            def _():
                step(d, scaled_delta_step(reach))

    def late_top(d, step):
        arrive(d, 1, False)
        step(d, top, False)

    late_deltas(late_top)

    def sum_delta(i):
        delta[i, 0:1, :] = functools.reduce(
            jnp.add, [stats[d, i, 3:4, :] * stats[d, i, 2:3, :] for d in range(reach + 1)]
        )

    sum_delta(top)
    over_near(top, grad_step)

    @pl.when(me >= reach)
    def _():
        grad_step(reach, top, False)

    finish(top)
    far_take(top, 1, 0)
    far_give(top, 1)

    if relayed:

        @pl.when(has_next)
        def _():
            for c in (1, 0):
                for k in range(1, pairs):
                    fetch(k, group, c).wait_recv()
                    relay(k, c).start()

    def late_rest(d, step):
        if d == reach:

            @pl.when(me >= reach)
            def _():
                last_hop(1).wait_recv()

        rest_blocks(d, step, top)

    def second_value(d, i, fresh):
        if isinstance(d, int):
            value_step(d, i, fresh)
        else:

            @pl.when((d < reach - 1) | (me < reach))
            def _():
                value_step(d, i, fresh)

    late_deltas(late_rest)
    for i in range(top):
        sum_delta(i)
    over_rest(reach, grad_step, top)
    send_first(reach, 0)
    far_take(top, 1, 1)
    over_near(second, second_value)
    over_near(second, grad_step)
    finish(second)
    far_take(second, 1, 0)
    far_give(second, 1)
    for d in range(reach - 1, 0, -1):

        @pl.when(me == d if d == reach - 1 else me >= d)
        def _():
            rest_blocks(d, value_step, second)

        if d < reach - 1:
            send_first(d, 1)
        if reach > 1:
            send_on(d, 1, me >= max(d, 2))
        over_rest(d, grad_step, second)
        send_first(d, 0)
        if d == reach - 1:
            far_take(second, 1, 1)
    over_rest(0, value_step, second)
    over_rest(0, grad_step, second)
    for i in range(second):
        finish(i)
    far_take(0, second, 0)
    far_give(0, second)
    far_take(0, second, 1)
    near_give()
    for d in range(reach - 1, 1, -1):
        send_on(d, 0)
    near_take()
    if reach > 1:
        send_on(1, 1, me == 1)
    if reach > 1:
        send_on(1, 0)
    settle(1)

    @pl.when(has_next)
    def _():
        for c in range(2):
            own_weights(c).wait()
            fetch(0, 1, c).wait_recv()
        near_adds(1)

    settle(0)

    @pl.when(has_next)
    def _():
        @pl.when(hold)
        def _():
            for k in range(1, pairs):
                to_far(k, 0, 1).start()

        for k in range(1, pairs):
            for c in range(2):
                if relayed:
                    relay(k, c, True).wait_recv()
                else:
                    for m in range(2):
                        fetch(k, m, c).wait_recv()
        far_passes(1)
        near_adds(0)
        far_adds(1)
        far_passes(0)
        far_adds(0)

    near = list(range(nb - 1, -1, -1))
    for c in near:
        for h in range(2):
            part = (slice(c * B, (c + 1) * B), slice(h * half_cols, (h + 1) * half_cols))
            value = near_sum[part]
            for k in range(1, pairs):
                to_far(k, c, h).wait_recv()
                value = value + far_in[k - 1, c, h].astype(jnp.float32)
            out_ref[part] = value.astype(jnp.bfloat16)

    @pl.when(has_next)
    def _():
        for k, m in others:
            for c in range(2):
                for n in range(2):
                    gather(k, m, c, n).wait_send()
        for item in fetches:
            fetch(*item).wait_send()
        if relayed:
            for k in range(1, pairs):
                for c in range(2):
                    relay(k, c).wait_send()

    for c in near:
        for h in range(2):
            for k in range(1, pairs):
                to_pair(k, c, h).wait_send()
                to_far(k, c, h).wait_send()
    for n in range(cols // piece):
        to_near(n).wait_send()

    for d in range(reach):

        @pl.when((me >= d) & has_next)
        def _():
            forward(d, 0).wait_send()
            if d == reach - 1:
                last_hop(0).wait_send()
                last_hop(1).wait_send()
            else:
                forward(d, 1).wait_send()

        @pl.when(me >= d + 1)
        def _():
            for c in range(2):
                for n in range(2):
                    backward(d + 1, c, n).wait_send()


def body(
    query,
    key_head_rows,
    value_head_rows,
    output_gradient,
    doc_blocks,
    w_query,
    key_weight,
    value_weight,
):
    shards = lax.axis_size("seq")
    places = lax.axis_size("tp")
    groups = lax.axis_size("groups")
    pairs = places // 2
    reach = min(8, shards - 1)
    rows, q_width = query.shape
    nb = rows // BLOCK_POSITIONS
    cols = w_query.shape[0] // places
    width = (q_width // HEAD_WIDTH) * BLOCK_POSITIONS
    half, full = jnp.bfloat16, jnp.float32
    vmem = pl.BlockSpec(memory_space=pltpu.VMEM)
    hbm = pl.BlockSpec(memory_space=pltpu.HBM)
    dma = pltpu.SemaphoreType.DMA
    buffers = [
        ((rows, q_width), half),
        ((rows, HEAD_WIDTH), half),
        ((rows, HEAD_WIDTH), half),
        ((rows, q_width), half),
        ((rows, q_width + 2 * HEAD_WIDTH), half),
        ((pairs - 1, 2, q_width + 2 * HEAD_WIDTH, cols), half),
        ((2, rows, 2 * pairs * HEAD_WIDTH), half),
        ((2, cols, 2 * pairs * HEAD_WIDTH), half),
        (w_query.shape, half),
        (key_weight.shape, half),
        (value_weight.shape, half),
        ((rows, cols), full),
        ((cols // math.gcd(cols, 512), rows, math.gcd(cols, 512)), half),
        ((cols // math.gcd(cols, 512), rows, math.gcd(cols, 512)), half),
        ((pairs - 1, nb, 2, rows // nb, cols // 2), half),
        ((pairs - 1, nb, 2, rows // nb, cols // 2), half),
        ((pairs - 1, nb, 2, rows // nb, cols // 2), half),
        ((pairs - 1, nb, 2, rows // nb, cols // 2), half),
    ]
    later = [
        ((reach, 2, rows, HEAD_WIDTH), half),
        ((nb, width, HEAD_WIDTH), half),
        ((nb, width, HEAD_WIDTH), half),
        ((reach + 1, nb, 8, width), full),
        ((nb, 8, width), full),
        ((nb, HEAD_WIDTH, width), full),
        ((reach + 1, nb, rows, width), half),
        ((reach + 1, 2, rows, HEAD_WIDTH), full),
        ((reach, 2, rows, HEAD_WIDTH), half),
        ((reach, 2, rows, HEAD_WIDTH), half),
    ]
    used = sum(math.prod(shape) * jnp.dtype(kind).itemsize for shape, kind in buffers + later)
    limit = min(used + SPARE_MIB * 1024 * 1024, 60 * 1024 * 1024)
    return pl.pallas_call(
        functools.partial(attention_kernel, shards, reach, places, groups),
        out_shape=jax.ShapeDtypeStruct((rows, cols), half),
        in_specs=[hbm] * 8,
        out_specs=vmem,
        scratch_shapes=[pltpu.SMEM(doc_blocks.shape, doc_blocks.dtype)]
        + [pltpu.VMEM(*item) for item in buffers]
        + [
            dma((5,)),
            dma((3,)),
            dma((cols // math.gcd(cols, 512),)),
            dma((cols // math.gcd(cols, 512),)),
            dma((pairs - 1, nb, 2)),
            dma((pairs - 1, nb, 2)),
            dma((pairs - 1, nb, 2)),
            dma((pairs - 1, nb, 2)),
            dma((pairs, 2, 2)),
            dma((pairs, 2, 2)),
            dma((pairs, 2)),
            dma((pairs, 2)),
            dma((pairs, 2, 2, 2)),
            dma((pairs, 2, 2, 2)),
        ]
        + [pltpu.VMEM(*item) for item in later]
        + [
            dma((reach, 2)),
            dma((reach, 2)),
            dma((2,)),
            dma((2,)),
            dma((reach, 2, 2)),
            dma((reach, 2, 2)),
        ],
        compiler_params=pltpu.CompilerParams(
            collective_id=0, has_side_effects=True, vmem_limit_bytes=limit
        ),
        name="attention",
    )(
        pltpu.with_memory_space_constraint(query, pltpu.HBM),
        pltpu.with_memory_space_constraint(key_head_rows, pltpu.HBM),
        pltpu.with_memory_space_constraint(value_head_rows, pltpu.HBM),
        pltpu.with_memory_space_constraint(output_gradient, pltpu.HBM),
        pltpu.with_memory_space_constraint(doc_blocks, pltpu.HBM),
        pltpu.with_memory_space_constraint(w_query, pltpu.HBM),
        pltpu.with_memory_space_constraint(key_weight, pltpu.HBM),
        pltpu.with_memory_space_constraint(value_weight, pltpu.HBM),
    )


def solution(mesh):
    in_specs = (
        P(("groups", "seq"), "tp"),
        P(("groups", "seq"), "tp"),
        P(("groups", "seq"), "tp"),
        P(("groups", "seq"), "tp"),
        P(("groups", "seq"), None),
        P(None, "tp"),
        P(None, "tp"),
        P(None, "tp"),
    )
    out_specs = P(("groups", "seq"), "tp")
    return jax.shard_map(body, mesh=mesh, in_specs=in_specs, out_specs=out_specs, check_vma=False)
```

```python
import functools
import math

import jax
import jax.numpy as jnp
from jax import lax
from jax.experimental import pallas as pl
from jax.experimental.pallas import tpu as pltpu
from jax.sharding import PartitionSpec as P

HEAD_WIDTH = 128
BLOCK_POSITIONS = 128
MESH_ID = pl.DeviceIdType.MESH
SPARE_MIB = 12


def dot_t(a, b):
    return lax.dot_general(a, b, (((1,), (1,)), ((), ())), preferred_element_type=jnp.float32)


def dot_n(a, b):
    return lax.dot_general(a, b, (((1,), (0,)), ((), ())), preferred_element_type=jnp.float32)


def dot_lt(a, b):
    return lax.dot_general(a, b, (((0,), (0,)), ((), ())), preferred_element_type=jnp.float32)


FLOOR = -1e9


def attention_kernel(
    shards,
    reach,
    places,
    groups,
    q_hbm,
    k_hbm,
    v_hbm,
    g_hbm,
    docs_hbm,
    wq_hbm,
    wk_hbm,
    wv_hbm,
    out_ref,
    docs_ref,
    q_ref,
    k_ref,
    v_ref,
    g_ref,
    dq_ref,
    turned_ref,
    dkv_all,
    kw_all,
    wq_ref,
    wk_ref,
    wv_ref,
    near_sum,
    near_out,
    near_in,
    pair_out,
    pair_in,
    far_out,
    far_in,
    load_sem,
    weight_sem,
    near_send,
    near_recv,
    pair_send,
    pair_recv,
    far_send,
    far_recv,
    fetch_send,
    fetch_recv,
    relay_send,
    relay_recv,
    gather_send,
    gather_recv,
    kv_win,
    q_heads,
    g_heads,
    stats,
    delta,
    dq_sum,
    probs,
    kv_sum,
    ret_out,
    ret_in,
    send_sem,
    recv_sem,
    last_send,
    last_recv,
    ret_send,
    ret_recv,
):
    B = BLOCK_POSITIONS
    rows = k_ref.shape[0]
    nb = rows // B
    heads = q_ref.shape[1] // HEAD_WIDTH
    lead = q_ref.shape[1]
    listed_count = docs_ref.shape[1]
    me = lax.axis_index("seq")
    scale = HEAD_WIDTH ** -0.5
    scale2 = scale * math.log2(math.e)
    has_next = me + 1 < shards
    has_prev = me >= 1

    pairs = places // 2
    place = lax.axis_index("tp")
    my_pair = place // 2
    parity = place % 2
    partner = my_pair * 2 + 1 - parity
    cols = out_ref.shape[1]
    relayed = groups == 2
    group = lax.axis_index("groups")

    def peer_of(k):
        return lax.rem(my_pair + k, pairs) * 2 + parity

    def owner_of(k, mine):
        return lax.rem(my_pair + k, pairs) * 2 + (parity if mine else 1 - parity)

    loads = [
        pltpu.make_async_copy(src, dst, load_sem.at[n])
        for n, (src, dst) in enumerate(((k_hbm, k_ref), (q_hbm, q_ref), (v_hbm, v_ref), (g_hbm, g_ref), (docs_hbm, docs_ref)))
    ]
    whole = [
        pltpu.make_async_copy(wq_hbm, wq_ref, weight_sem.at[0]),
        pltpu.make_async_copy(wk_hbm, wk_ref, weight_sem.at[1]),
        pltpu.make_async_copy(wv_hbm, wv_ref, weight_sem.at[2]),
    ]
    for copy in loads + whole:
        copy.start()

    barrier = pltpu.get_barrier_semaphore()
    others = [(k, m) for k in range(pairs) for m in range(2) if (k, m) != (0, 0)]
    for k, m in others:
        pl.semaphore_signal(barrier, inc=1, device_id={"tp": owner_of(k, m == 0)}, device_id_type=MESH_ID)
    if relayed:
        pl.semaphore_signal(barrier, inc=1, device_id={"groups": 1 - group}, device_id_type=MESH_ID)

    @pl.when(has_next)
    def _():
        pl.semaphore_signal(barrier, inc=1, device_id={"seq": me + 1}, device_id_type=MESH_ID)

    @pl.when(has_prev)
    def _():
        pl.semaphore_signal(barrier, inc=1, device_id={"seq": me - 1}, device_id_type=MESH_ID)

    greeted = places - 1 + (1 if relayed else 0)
    pl.semaphore_wait(barrier, has_next.astype(jnp.int32) + has_prev.astype(jnp.int32) + greeted)

    def forward(d, c):
        src = (k_hbm, v_hbm)[c] if d == 0 else kv_win.at[d - 1, c]
        return pltpu.make_async_remote_copy(
            src_ref=src,
            dst_ref=kv_win.at[d, c],
            send_sem=send_sem.at[d, c],
            recv_sem=recv_sem.at[d, c],
            device_id={"seq": jnp.minimum(me + 1, shards - 1)},
            device_id_type=MESH_ID,
        )

    def last_hop(n):
        span = pl.ds(rows - B, B) if n == 0 else pl.ds(0, rows - B)
        return pltpu.make_async_remote_copy(
            src_ref=(v_hbm if reach == 1 else kv_win.at[reach - 2, 1]).at[span],
            dst_ref=kv_win.at[reach - 1, 1, span],
            send_sem=last_send.at[n],
            recv_sem=last_recv.at[n],
            device_id={"seq": jnp.minimum(me + 1, shards - 1)},
            device_id_type=MESH_ID,
        )

    spans = [slice(n * (rows // 2), (n + 1) * (rows // 2)) for n in range(2)]

    def backward(d, c, n):
        return pltpu.make_async_remote_copy(
            src_ref=ret_out.at[d - 1, c, spans[n]],
            dst_ref=ret_in.at[d - 1, c, spans[n]],
            send_sem=ret_send.at[d - 1, c, n],
            recv_sem=ret_recv.at[d - 1, c, n],
            device_id={"seq": jnp.maximum(me - 1, 0)},
            device_id_type=MESH_ID,
        )

    def span_of(owner):
        return pl.ds(pl.multiple_of(owner * cols, cols), cols)

    def slot(k, m):
        lane = (2 * k + m) * HEAD_WIDTH
        return pl.ds(lane if isinstance(m, int) else pl.multiple_of(lane, HEAD_WIDTH), HEAD_WIDTH)

    def fetch(k, m, c):
        if isinstance(m, int):
            owner = owner_of(k, m == 0)
        else:
            owner = lax.rem(my_pair + k, pairs) * 2 + lax.rem(parity + m, 2)
        return pltpu.make_async_remote_copy(
            src_ref=(wk_hbm, wv_hbm)[c].at[span_of(owner)],
            dst_ref=kw_all.at[c, :, slot(k, m)],
            send_sem=fetch_send.at[k, m, c],
            recv_sem=fetch_recv.at[k, m, c],
            device_id={"tp": owner},
            device_id_type=MESH_ID,
        )

    def own_weights(c):
        return pltpu.make_async_copy(
            (wk_hbm, wv_hbm)[c].at[span_of(place)], kw_all.at[c, :, slot(0, 0)], fetch_recv.at[0, 0, c]
        )

    def relay(k, c, arriving=False):
        which = 1 - group if arriving else group
        return pltpu.make_async_remote_copy(
            src_ref=kw_all.at[c, :, slot(k, which)],
            dst_ref=kw_all.at[c, :, slot(k, which)],
            send_sem=relay_send.at[k, c],
            recv_sem=relay_recv.at[k, c],
            device_id={"groups": 1 - group},
            device_id_type=MESH_ID,
        )

    if relayed:
        fetches = [(0, 1, c) for c in range(2)] + [(k, group, c) for c in (1, 0) for k in range(1, pairs)]
    else:
        fetches = [(k, m, c) for k, m in others for c in range(2)]

    @pl.when(has_next)
    def _():
        forward(0, 0).start()

        @pl.when((me != 1) | (parity == 0))
        def _():
            forward(0, 1).start()

        for item in fetches:
            fetch(*item).start()
        for c in range(2):
            own_weights(c).start()

    width = heads * B
    for d in range(1, reach + 1):
        for i in range(nb):
            stats[d, i, 0:1, :] = jnp.full((1, width), FLOOR, jnp.float32)
            stats[d, i, 1:3, :] = jnp.zeros((2, width), jnp.float32)

    for i in range(nb):
        dq_sum[i] = jnp.zeros((HEAD_WIDTH, width), jnp.float32)

    @pl.when(me >= reach)
    def _():
        kv_sum[reach, 0] = jnp.zeros((rows, HEAD_WIDTH), jnp.float32)

    for copy in loads:
        copy.wait()
    for i in range(nb):
        for h in range(heads):
            q_heads[i, h * B : (h + 1) * B, :] = q_ref[i * B : (i + 1) * B, h * HEAD_WIDTH : (h + 1) * HEAD_WIDTH]
            g_heads[i, h * B : (h + 1) * B, :] = g_ref[i * B : (i + 1) * B, h * HEAD_WIDTH : (h + 1) * HEAD_WIDTH]
    key_row = lax.broadcasted_iota(jnp.int32, (B, width), 0)
    query_row = lax.broadcasted_iota(jnp.int32, (B, width), 1) & (B - 1)
    own_mask = key_row <= query_row

    def keys_of(d):
        if isinstance(d, int) and d == 0:
            return k_ref, v_ref
        return kv_win.at[d - 1, 0], kv_win.at[d - 1, 1]

    def key_span(d, i):
        if isinstance(i, int) and isinstance(d, int) and d == 0:
            return 0, i + 1
        if isinstance(i, int) and isinstance(d, int) and d == reach:
            return i, nb
        return 0, nb

    def biased(d, i, j, raw):
        offset = d * nb + i - j
        if isinstance(i, int) and offset == 0:
            return jnp.where(own_mask, raw, -jnp.inf), jnp.float32(0.0)
        if isinstance(i, int) and offset == 1:
            return jnp.where(own_mask, -jnp.inf, raw), jnp.float32(0.0)
        key_block = (me - d) * nb + j
        hits = jnp.int32(0)
        for n in range(listed_count):
            hits = hits | (docs_ref[i, n] == key_block).astype(jnp.int32)
        ok = (hits > 0) & (offset >= 2)
        return raw, jnp.where(ok, jnp.float32(0.0), jnp.float32(-jnp.inf))

    def raw_blocks(d, i):
        low, high = key_span(d, i)
        raw = dot_t(keys_of(d)[0][low * B : high * B, :], q_heads[i])
        return [
            biased(d, i, j, raw[(j - low) * B : (j - low + 1) * B]) for j in range(low, high)
        ]

    def score_step(d, i, fresh):
        low, high = key_span(d, i)
        blocks = raw_blocks(d, i)
        tops = [jnp.max(raw, axis=0, keepdims=True) * scale2 + bias for raw, bias in blocks]
        top = jnp.maximum(functools.reduce(jnp.maximum, tops), FLOOR)
        total = 0.0
        for j, (raw, bias) in enumerate(blocks):
            weight = jnp.exp2(raw * scale2 + (bias - top))
            total = total + jnp.sum(weight, axis=0, keepdims=True)
            probs[d, i, (low + j) * B : (low + j + 1) * B, :] = weight.astype(jnp.bfloat16)
        stats[d, i, 0:1, :] = top
        stats[d, i, 1:2, :] = total

    def delta_step(d, i, fresh):
        low, high = key_span(d, i)
        prob_grad = dot_t(keys_of(d)[1][low * B : high * B, :], g_heads[i])
        weight = probs[d, i, low * B : high * B, :].astype(jnp.float32)
        stats[d, i, 2:3, :] = jnp.sum(weight * prob_grad, axis=0, keepdims=True)

    def scaled_delta_step(whole_from):
        def step(d, i, fresh):
            delta_step(d, i, fresh)
            done = jnp.logical_or(jnp.int32(d) >= whole_from, jnp.int32(i) == nb - 1)
            stats[d, i, 3:4, :] = jnp.where(done, jnp.float32(1.0), stats[d, i, 1:2, :])

        return step

    def value_step(d, i, fresh):
        low, high = key_span(d, i)
        weight = probs[d, i, low * B : high * B, :].astype(jnp.float32)
        prob_half = (weight * stats[d, i, 1:2, :]).astype(jnp.bfloat16)
        probs[d, i, low * B : high * B, :] = prob_half
        term = dot_n(prob_half, g_heads[i])
        if fresh:
            kv_sum[d, 1, low * B : high * B, :] = term
        else:
            kv_sum[d, 1, low * B : high * B, :] += term

    def grad_step(d, i, fresh):
        low, high = key_span(d, i)
        keys = keys_of(d)[0][low * B : high * B, :]
        prob_grad = dot_t(keys_of(d)[1][low * B : high * B, :], g_heads[i])
        prob = probs[d, i, low * B : high * B, :].astype(jnp.float32)
        score_half = (prob * (prob_grad - delta[i, 0:1, :])).astype(jnp.bfloat16)
        term = dot_n(score_half, q_heads[i])
        if fresh:
            kv_sum[d, 0, low * B : high * B, :] = term
        else:
            kv_sum[d, 0, low * B : high * B, :] += term
        dq_sum[i] += dot_lt(keys, score_half)

    def over_blocks(d, step):
        if d == 0:
            for i in range(nb - 1, -1, -1):
                step(d, i, i == nb - 1)
            return
        step(d, 0, True)
        if d == reach:
            for i in range(1, nb):
                step(d, i, False)
            return

        def one(i, carry):
            step(d, i, False)
            return carry

        lax.fori_loop(1, nb, one, 0)

    def present(d, step, extra=None):
        @pl.when(me >= d if extra is None else (me >= d) & extra)
        def _():
            over_blocks(d, step)

    def arrive(d, c, checked=True):
        there = me >= d if checked else True

        @pl.when(there)
        def _():
            if (d, c) == (reach, 1):
                last_hop(0).wait_recv()
            else:
                forward(d - 1, c).wait_recv()

        if d < reach:

            @pl.when(there & has_next)
            def _():
                if (d, c) == (reach - 1, 1):
                    last_hop(0).start()
                    last_hop(1).start()
                else:
                    forward(d, c).start()

    def take_values(d, step):
        arrive(d, 1, False)
        over_blocks(d, step)

    def scaled(d, c, n):
        return kv_sum[d, c, spans[n]] * scale if c == 0 else kv_sum[d, c, spans[n]]

    def send_first(d, c, extra=True):
        first = me >= d if d == reach else (me >= d) & jnp.logical_not(has_next) & extra

        @pl.when(first)
        def _():
            for n in range(2):
                ret_out[d - 1, c, spans[n]] = scaled(d, c, n).astype(jnp.bfloat16)
                backward(d, c, n).start()

    def send_on(d, c, extra=None):
        @pl.when((me >= d if extra is None else extra) & has_next)
        def _():
            for n in range(2):
                backward(d + 1, c, n).wait_recv()
                total = scaled(d, c, n) + ret_in[d, c, spans[n]].astype(jnp.float32)
                ret_out[d - 1, c, spans[n]] = total.astype(jnp.bfloat16)
                backward(d, c, n).start()

    present(0, score_step)
    present(0, delta_step)
    for copy in whole:
        copy.wait()
    for k in range(1, pairs):
        for m in range(2):
            span = span_of(owner_of(k, m == 0))
            turned_ref[k - 1, m, :lead, :] = wq_ref[span, :].T

    @pl.when(jnp.logical_not(has_next))
    def _():
        for k in range(1, pairs):
            for m in range(2):
                span = span_of(owner_of(k, m == 0))
                turned_ref[k - 1, m, lead : lead + HEAD_WIDTH, :] = wk_ref[span, :].T
                turned_ref[k - 1, m, lead + HEAD_WIDTH :, :] = wv_ref[span, :].T

    for d in range(1, reach + 1):
        arrive(d, 0)
        present(d, score_step)
        if d == 1:

            @pl.when((me == 1) & (parity == 1) & has_next)
            def _():
                forward(0, 1).start()

        if d < reach:

            @pl.when(me > d + 1)
            def _():
                take_values(d, delta_step)

    for i in range(nb):
        tops = [stats[d, i, 0:1, :] for d in range(reach + 1)]
        top = functools.reduce(jnp.maximum, tops)
        parts = [jnp.exp2(t - top) for t in tops]
        total = functools.reduce(jnp.add, [parts[d] * stats[d, i, 1:2, :] for d in range(reach + 1)])
        inverse = 1.0 / total
        for d in range(reach + 1):
            stats[d, i, 1:2, :] = parts[d] * inverse
            stats[d, i, 3:4, :] = parts[d] * inverse

    top, second = nb - 1, nb - 2

    def over_near(i, step):
        step(0, i, i == top)

        def one(d, carry):
            step(d, i, i == top)
            return carry

        if reach > 1:
            lax.fori_loop(1, jnp.minimum(me, reach - 1) + 1, one, 0)

    def rest_blocks(d, step, count):
        if d in (0, reach):
            for i in range(count - 1, -1, -1):
                step(d, i, False)
            return

        if reach <= 3 and count <= 2:
            for i in range(count):
                step(d, i, False)
            return

        def one(i, carry):
            step(d, i, False)
            return carry

        lax.fori_loop(0, count, one, 0)

    def over_rest(d, step, count):
        @pl.when(me >= d)
        def _():
            rest_blocks(d, step, count)

    def finish(i):
        part = slice(i * B, (i + 1) * B)
        turned = (dq_sum[i] * scale).T.astype(jnp.bfloat16)
        for h in range(heads):
            dq_ref[part, h * HEAD_WIDTH : (h + 1) * HEAD_WIDTH] = turned[h * B : (h + 1) * B]

        @pl.when(jnp.logical_not(has_next))
        def _():
            for c in range(2):
                own = kv_sum[0, c, part, :] * scale if c == 0 else kv_sum[0, c, part, :]
                dq_ref[part, lead + c * HEAD_WIDTH : lead + (c + 1) * HEAD_WIDTH] = own.astype(jnp.bfloat16)

    half_cols = cols // 2
    piece = math.gcd(cols, 512)
    hold = me + 2 == shards

    def term(owner, part, first, count, keep):
        span = pl.ds(pl.multiple_of(owner * cols + first, count), count)
        value = dot_t(dq_ref[part, :lead], wq_ref[span, :])
        if keep:
            value = value + dot_t(dq_ref[part, lead : lead + HEAD_WIDTH], wk_ref[span, :])
            value = value + dot_t(dq_ref[part, lead + HEAD_WIDTH :], wv_ref[span, :])
        return value

    def far_term(k, m, part, keep):
        depth = lead + 2 * HEAD_WIDTH if keep else lead
        return dot_n(dq_ref[part, :depth], turned_ref[k - 1, m, :depth, :])

    def to_pair(k, c, h):
        return pltpu.make_async_remote_copy(
            src_ref=pair_out.at[k - 1, c, h],
            dst_ref=pair_in.at[k - 1, c, h],
            send_sem=pair_send.at[k - 1, c, h],
            recv_sem=pair_recv.at[k - 1, c, h],
            device_id={"tp": partner},
            device_id_type=MESH_ID,
        )

    def to_far(k, c, h):
        return pltpu.make_async_remote_copy(
            src_ref=far_out.at[k - 1, c, h],
            dst_ref=far_in.at[k - 1, c, h],
            send_sem=far_send.at[k - 1, c, h],
            recv_sem=far_recv.at[k - 1, c, h],
            device_id={"tp": peer_of(k)},
            device_id_type=MESH_ID,
        )

    def to_near(n):
        return pltpu.make_async_remote_copy(
            src_ref=near_out.at[n],
            dst_ref=near_in.at[n],
            send_sem=near_send.at[n],
            recv_sem=near_recv.at[n],
            device_id={"tp": partner},
            device_id_type=MESH_ID,
        )

    def both(step):
        @pl.when(has_next)
        def _():
            step(False)

        @pl.when(jnp.logical_not(has_next))
        def _():
            step(True)

    def far_give(low, count):
        part = slice(low * B, (low + count) * B)

        def step(keep):
            for k in range(1, pairs):
                value = far_term(k, 1, part, keep).astype(jnp.bfloat16)
                for n in range(count - 1, -1, -1):
                    for h in range(2):
                        pair_out[k - 1, low + n, h] = value[n * B : (n + 1) * B, h * half_cols : (h + 1) * half_cols]
                        to_pair(k, low + n, h).start()

        both(step)

    def far_take(low, count, which):
        part = slice(low * B, (low + count) * B)

        def step(keep):
            for k in range(1, pairs):
                value = far_term(k, 0, part, keep)
                for n in range(count - 1, -1, -1):
                    for h in range(2):
                        c = low + n
                        to_pair(k, c, h).wait_recv()
                        total = value[n * B : (n + 1) * B, h * half_cols : (h + 1) * half_cols]
                        total = total + pair_in[k - 1, c, h].astype(jnp.float32)
                        far_out[k - 1, c, h] = total.astype(jnp.bfloat16)
                        if keep or (c, h) != (0, 1):
                            to_far(k, c, h).start()
                        else:

                            @pl.when(jnp.logical_not(hold))
                            def _():
                                to_far(k, c, h).start()

        @pl.when(parity == which)
        def _():
            both(step)

    def near_give():
        def step(keep):
            for n in range(cols // piece):
                near_out[n] = term(partner, slice(0, rows), n * piece, piece, keep).astype(jnp.bfloat16)
                to_near(n).start()

        both(step)

    def near_take():
        def step(keep):
            for n in range(cols // piece):
                value = term(place, slice(0, rows), n * piece, piece, keep)
                to_near(n).wait_recv()
                near_sum[:, n * piece : (n + 1) * piece] = value + near_in[n].astype(jnp.float32)

        both(step)

    def gather(k, m, c, n):
        return pltpu.make_async_remote_copy(
            src_ref=dkv_all.at[c, spans[n], slot(k, 0)] if m == 1 else dkv_all.at[c, spans[n], slot(0, 0)],
            dst_ref=dkv_all.at[c, spans[n], slot(k, m)],
            send_sem=gather_send.at[k, m, c, n],
            recv_sem=gather_recv.at[k, m, c, n],
            device_id={"tp": partner if m == 1 else peer_of(k)},
            device_id_type=MESH_ID,
        )

    def settle(c, extra=True):
        @pl.when(has_next & extra)
        def _():
            for n in range(2):
                backward(1, c, n).wait_recv()
                total = scaled(0, c, n) + ret_in[0, c, spans[n]].astype(jnp.float32)
                dkv_all[c, spans[n], 0:HEAD_WIDTH] = total.astype(jnp.bfloat16)
                for k in range(1, pairs):
                    gather(k, 0, c, n).start()
            for n in range(2):
                gather(0, 1, c, n).start()

    def add_terms(k, c):
        lanes = slice(2 * k * HEAD_WIDTH, (2 * k + 2) * HEAD_WIDTH)
        step_cols = min(256, cols)
        for n in range(0, cols, step_cols):
            near_sum[:, n : n + step_cols] += dot_t(dkv_all[c, :, lanes], kw_all[c, n : n + step_cols, lanes])

    def near_adds(c):
        for n in range(2):
            gather(0, 1, c, n).wait_recv()
        add_terms(0, c)

    def far_passes(c):
        for k in range(1, pairs):
            for n in range(2):
                gather(k, 0, c, n).wait_recv()
                gather(k, 1, c, n).start()

    def far_adds(c):
        for k in range(1, pairs):
            for n in range(2):
                gather(k, 1, c, n).wait_recv()
            add_terms(k, c)

    present(reach, value_step)
    send_first(reach, 1)
    over_near(top, value_step)


    if reach > 1:

        @pl.when(me >= reach)
        def _():
            rest_blocks(reach - 1, value_step, top)

        send_first(reach - 1, 1, me >= reach)

    def late_deltas(step):
        for d in range(1, reach):

            @pl.when(me == d + 1)
            def _():
                step(d, scaled_delta_step(reach - 1 if d == reach - 1 else reach))

        for d in range(1, reach + 1):

            @pl.when(me >= reach if d == reach else me == d)
            def _():
                step(d, scaled_delta_step(reach))

    def late_top(d, step):
        arrive(d, 1, False)
        step(d, top, False)

    late_deltas(late_top)

    def sum_delta(i):
        delta[i, 0:1, :] = functools.reduce(
            jnp.add, [stats[d, i, 3:4, :] * stats[d, i, 2:3, :] for d in range(reach + 1)]
        )

    sum_delta(top)
    over_near(top, grad_step)

    @pl.when(me >= reach)
    def _():
        grad_step(reach, top, False)

    finish(top)
    far_take(top, 1, 0)
    far_give(top, 1)

    if relayed:

        @pl.when(has_next)
        def _():
            for c in (1, 0):
                for k in range(1, pairs):
                    fetch(k, group, c).wait_recv()
                    relay(k, c).start()

    def late_rest(d, step):
        if d == reach:

            @pl.when(me >= reach)
            def _():
                last_hop(1).wait_recv()

        rest_blocks(d, step, top)

    def second_value(d, i, fresh):
        if isinstance(d, int):
            value_step(d, i, fresh)
        else:

            @pl.when((d < reach - 1) | (me < reach))
            def _():
                value_step(d, i, fresh)

    late_deltas(late_rest)
    for i in range(top):
        sum_delta(i)
    over_rest(reach, grad_step, top)
    send_first(reach, 0)
    far_take(top, 1, 1)
    over_near(second, second_value)
    over_near(second, grad_step)
    finish(second)
    far_take(second, 1, 0)
    far_give(second, 1)
    for d in range(reach - 1, 0, -1):

        @pl.when(me == d if d == reach - 1 else me >= d)
        def _():
            rest_blocks(d, value_step, second)

        if d < reach - 1:
            send_first(d, 1)
        if reach > 1:
            send_on(d, 1, me >= max(d, 2))
        over_rest(d, grad_step, second)
        send_first(d, 0)
        if d == reach - 1:
            far_take(second, 1, 1)
    over_rest(0, value_step, second)
    over_rest(0, grad_step, second)
    for i in range(second):
        finish(i)
    far_give(0, second)
    far_take(0, second, 0)
    far_take(0, second, 1)
    near_give()
    for d in range(reach - 1, 1, -1):
        send_on(d, 0)
    near_take()
    if reach > 1:
        send_on(1, 1, me == 1)
    if reach > 1:
        send_on(1, 0)
    settle(1)

    @pl.when(has_next)
    def _():
        for c in range(2):
            own_weights(c).wait()
            fetch(0, 1, c).wait_recv()
        near_adds(1)

    settle(0)

    @pl.when(has_next)
    def _():
        @pl.when(hold)
        def _():
            for k in range(1, pairs):
                to_far(k, 0, 1).start()

        for k in range(1, pairs):
            for c in range(2):
                if relayed:
                    relay(k, c, True).wait_recv()
                else:
                    for m in range(2):
                        fetch(k, m, c).wait_recv()
        far_passes(1)
        near_adds(0)
        far_adds(1)
        far_passes(0)
        far_adds(0)

    near = list(range(nb - 1, -1, -1))
    for c in near:
        for h in range(2):
            part = (slice(c * B, (c + 1) * B), slice(h * half_cols, (h + 1) * half_cols))
            value = near_sum[part]
            for k in range(1, pairs):
                to_far(k, c, h).wait_recv()
                value = value + far_in[k - 1, c, h].astype(jnp.float32)
            out_ref[part] = value.astype(jnp.bfloat16)

    @pl.when(has_next)
    def _():
        for k, m in others:
            for c in range(2):
                for n in range(2):
                    gather(k, m, c, n).wait_send()
        for item in fetches:
            fetch(*item).wait_send()
        if relayed:
            for k in range(1, pairs):
                for c in range(2):
                    relay(k, c).wait_send()

    for c in near:
        for h in range(2):
            for k in range(1, pairs):
                to_pair(k, c, h).wait_send()
                to_far(k, c, h).wait_send()
    for n in range(cols // piece):
        to_near(n).wait_send()

    for d in range(reach):

        @pl.when((me >= d) & has_next)
        def _():
            forward(d, 0).wait_send()
            if d == reach - 1:
                last_hop(0).wait_send()
                last_hop(1).wait_send()
            else:
                forward(d, 1).wait_send()

        @pl.when(me >= d + 1)
        def _():
            for c in range(2):
                for n in range(2):
                    backward(d + 1, c, n).wait_send()


def body(
    query,
    key_head_rows,
    value_head_rows,
    output_gradient,
    doc_blocks,
    w_query,
    key_weight,
    value_weight,
):
    shards = lax.axis_size("seq")
    places = lax.axis_size("tp")
    groups = lax.axis_size("groups")
    pairs = places // 2
    reach = min(8, shards - 1)
    rows, q_width = query.shape
    nb = rows // BLOCK_POSITIONS
    cols = w_query.shape[0] // places
    width = (q_width // HEAD_WIDTH) * BLOCK_POSITIONS
    half, full = jnp.bfloat16, jnp.float32
    vmem = pl.BlockSpec(memory_space=pltpu.VMEM)
    hbm = pl.BlockSpec(memory_space=pltpu.HBM)
    dma = pltpu.SemaphoreType.DMA
    buffers = [
        ((rows, q_width), half),
        ((rows, HEAD_WIDTH), half),
        ((rows, HEAD_WIDTH), half),
        ((rows, q_width), half),
        ((rows, q_width + 2 * HEAD_WIDTH), half),
        ((pairs - 1, 2, q_width + 2 * HEAD_WIDTH, cols), half),
        ((2, rows, 2 * pairs * HEAD_WIDTH), half),
        ((2, cols, 2 * pairs * HEAD_WIDTH), half),
        (w_query.shape, half),
        (key_weight.shape, half),
        (value_weight.shape, half),
        ((rows, cols), full),
        ((cols // math.gcd(cols, 512), rows, math.gcd(cols, 512)), half),
        ((cols // math.gcd(cols, 512), rows, math.gcd(cols, 512)), half),
        ((pairs - 1, nb, 2, rows // nb, cols // 2), half),
        ((pairs - 1, nb, 2, rows // nb, cols // 2), half),
        ((pairs - 1, nb, 2, rows // nb, cols // 2), half),
        ((pairs - 1, nb, 2, rows // nb, cols // 2), half),
    ]
    later = [
        ((reach, 2, rows, HEAD_WIDTH), half),
        ((nb, width, HEAD_WIDTH), half),
        ((nb, width, HEAD_WIDTH), half),
        ((reach + 1, nb, 8, width), full),
        ((nb, 8, width), full),
        ((nb, HEAD_WIDTH, width), full),
        ((reach + 1, nb, rows, width), half),
        ((reach + 1, 2, rows, HEAD_WIDTH), full),
        ((reach, 2, rows, HEAD_WIDTH), half),
        ((reach, 2, rows, HEAD_WIDTH), half),
    ]
    used = sum(math.prod(shape) * jnp.dtype(kind).itemsize for shape, kind in buffers + later)
    limit = min(used + SPARE_MIB * 1024 * 1024, 60 * 1024 * 1024)
    return pl.pallas_call(
        functools.partial(attention_kernel, shards, reach, places, groups),
        out_shape=jax.ShapeDtypeStruct((rows, cols), half),
        in_specs=[hbm] * 8,
        out_specs=vmem,
        scratch_shapes=[pltpu.SMEM(doc_blocks.shape, doc_blocks.dtype)]
        + [pltpu.VMEM(*item) for item in buffers]
        + [
            dma((5,)),
            dma((3,)),
            dma((cols // math.gcd(cols, 512),)),
            dma((cols // math.gcd(cols, 512),)),
            dma((pairs - 1, nb, 2)),
            dma((pairs - 1, nb, 2)),
            dma((pairs - 1, nb, 2)),
            dma((pairs - 1, nb, 2)),
            dma((pairs, 2, 2)),
            dma((pairs, 2, 2)),
            dma((pairs, 2)),
            dma((pairs, 2)),
            dma((pairs, 2, 2, 2)),
            dma((pairs, 2, 2, 2)),
        ]
        + [pltpu.VMEM(*item) for item in later]
        + [
            dma((reach, 2)),
            dma((reach, 2)),
            dma((2,)),
            dma((2,)),
            dma((reach, 2, 2)),
            dma((reach, 2, 2)),
        ],
        compiler_params=pltpu.CompilerParams(
            collective_id=0, has_side_effects=True, vmem_limit_bytes=limit
        ),
        name="attention",
    )(
        pltpu.with_memory_space_constraint(query, pltpu.HBM),
        pltpu.with_memory_space_constraint(key_head_rows, pltpu.HBM),
        pltpu.with_memory_space_constraint(value_head_rows, pltpu.HBM),
        pltpu.with_memory_space_constraint(output_gradient, pltpu.HBM),
        pltpu.with_memory_space_constraint(doc_blocks, pltpu.HBM),
        pltpu.with_memory_space_constraint(w_query, pltpu.HBM),
        pltpu.with_memory_space_constraint(key_weight, pltpu.HBM),
        pltpu.with_memory_space_constraint(value_weight, pltpu.HBM),
    )


def solution(mesh):
    in_specs = (
        P(("groups", "seq"), "tp"),
        P(("groups", "seq"), "tp"),
        P(("groups", "seq"), "tp"),
        P(("groups", "seq"), "tp"),
        P(("groups", "seq"), None),
        P(None, "tp"),
        P(None, "tp"),
        P(None, "tp"),
    )
    out_specs = P(("groups", "seq"), "tp")
    return jax.shard_map(body, mesh=mesh, in_specs=in_specs, out_specs=out_specs, check_vma=False)
```
